256 devices in a mesh: eval: 64 (over z, y, core), blk: 4 (over x).
Axes of the slice: x: 4, y: 4, z: 8, core: 2. Of those that a mesh axis runs over, the one named last changes fastest.
Arguments:
- sample_occ: int32 [1024, 2, 256], P(('eval', 'blk')), may hold values 0 or 1
- unique_occ: int32 [8192, 2, 256], P(('eval', 'blk')), may hold values 0 or 1
- conn_index: int32 [1024, 32], P(('eval', 'blk')), may hold values from 0 to 8191
- hop_sign: int32 [1024, 32], P(('eval', 'blk')), may hold values from 0 to 1
- gram_owner: int32 [256], replicated, may hold values from 0 to 255, each once
- embed: float32 [3, 256], replicated, may hold values from -6 to 6
- kernels: float32 [2, 25, 256], replicated, may hold values from -5 to 5
- weights: bfloat16 [2, 256, 256], replicated, may hold values from -0.375 to 0.375
- biases: float32 [2, 256], replicated, may hold values from -3 to 3
- readout: float32 [256], replicated, may hold values from -0.0234375 to 0.0234375
Outputs:
- local_energy: float32 [1024], P(('eval', 'blk'))
- gram: float32 [1024, 1024], P(('eval', 'blk'))
- force: float32 [65536], P(('eval', 'blk'))
The draws below stay inside these ranges and needn't reach their ends.
Inputs may be any that keep to these rules, and one draw needn't show every extreme that they name: `sample_occ`: 1 marks an occupied spin orbital. `unique_occ`: 1 marks an occupied spin orbital. `conn_index`: indices into the unique configurations, in their order over the devices. `hop_sign`: 1 for a positive, 0 for a negative matrix element. `gram_owner`: a permutation of the device indices.
All inputs are finite; a program needn't handle non-finite values. No bound on the sum of `sample_occ` or of `unique_occ` on one device may be relied on, other than what follows from the above.
Results may differ from the reference program's by a relative error of at most 0.024.
Values may be sent and summed in bfloat16 or wider, within the bound.
A program may use at most 64 MiB of HBM per device.

```python
import math
import jax
import jax.numpy as jnp
import numpy as np
from jax import lax

LAT = 16
CH = 256
KSIZE = 5
LAYERS = 2
K = 32
S_DEV = 4
U_DEV = 32
SITES = 256
N_S = 1024
U_TOTAL = 8192
DEVICES = 256


def draw_kernels(key, part):
    first = jax.random.fold_in(key, 11)
    second = jax.random.fold_in(key, 23)
    base = jnp.clip(jax.random.normal(first, (LAYERS, KSIZE * KSIZE, CH), jnp.float32), -6.0, 6.0)
    factor = jnp.exp(jax.random.uniform(second, (LAYERS, 1, CH), jnp.float32, math.log(0.25), math.log(4.0)))
    return base * factor / KSIZE


def set_ends(result, rng, low, largest):
    index_at = [jax.random.randint(jax.random.fold_in(rng, axis), (), 0, length) for axis, length in enumerate(result.shape)]
    main_axis = result.shape.index(max(result.shape))
    next_to = index_at[:main_axis] + [(index_at[main_axis] + 1) % result.shape[main_axis]] + index_at[main_axis + 1:]
    return result.at[tuple(index_at)].set(low).at[tuple(next_to)].set(largest)


def rank_table(count, lean):
    loads = [(1 << 20) // math.isqrt(standing ** lean) + 1 for standing in range(1, count + 1)]
    spread = 1 + sum(loads) // (1 << 30)
    return np.cumsum(np.array([max(1, weight // spread) for weight in loads]))


def ranked(own_key, dims, number_of, skew):
    listing = rank_table(number_of, skew)
    lot = jax.random.randint(jax.random.fold_in(own_key, 1), dims, 0, int(listing[number_of - 1]))
    rank = jnp.searchsorted(jnp.asarray(listing, jnp.int32), lot, side="right")
    return jax.random.permutation(jax.random.fold_in(own_key, 2), number_of)[rank].astype(jnp.int32)


def noise(key, extent, spread, limit, held_as=jnp.bfloat16):
    entries = spread * jax.random.normal(key, extent, jnp.float32)
    return jnp.clip(entries, min=-limit, max=limit).astype(held_as)


def setup_inputs(seed: int = 0) -> dict:
    key_of = jax.random.split(jax.random.key(seed), 11)
    return {
        "sample_occ": set_ends((jax.random.randint(key_of[0], (N_S, 2, SITES), 0, 2) < 1).astype(jnp.int32), jax.random.fold_in(key_of[0], 1), 0, 1),
        "unique_occ": set_ends((jax.random.randint(key_of[1], (U_TOTAL, 2, SITES), 0, 2) < 1).astype(jnp.int32), jax.random.fold_in(key_of[1], 1), 0, 1),
        "conn_index": set_ends(ranked(key_of[2], (N_S, K), U_TOTAL, 1), jax.random.fold_in(key_of[2], 3), 0, U_TOTAL - 1).astype(jnp.int32),
        "hop_sign": set_ends(jax.random.randint(key_of[3], (N_S, K), 0, 2), jax.random.fold_in(key_of[3], 1), 0, 1).astype(jnp.int32),
        "gram_owner": jax.random.permutation(key_of[4], DEVICES).astype(jnp.int32),
        "embed": noise(key_of[5], (3, CH), 1.0, 6.0, jnp.float32),
        "kernels": draw_kernels(jax.random.fold_in(key_of[10], 71), 0),
        "weights": noise(key_of[7], (LAYERS, CH, CH), CH ** -0.5, 0.375),
        "biases": noise(key_of[8], (LAYERS, CH), 0.5, 3.0, jnp.float32),
        "readout": noise(key_of[9], (CH,), (SITES * CH) ** -0.5, 0.0234375, jnp.float32),
    }


HOP = 1.0
INTER = 4.0


def depthwise(grid, kernel):
    reach = KSIZE // 2
    side = grid.shape[1]
    padded = jnp.pad(grid, ((0, 0), (reach, reach), (reach, reach), (0, 0)), mode="wrap")
    total = jnp.zeros_like(grid)
    for row_off in range(KSIZE):
        for col_off in range(KSIZE):
            total = total + padded[:, row_off:row_off + side, col_off:col_off + side, :] * kernel[row_off * KSIZE + col_off]
    return total


def network(occ, embed, kernels, weights, biases, readout):
    count = occ.shape[0]
    cells = occ.shape[2]
    filled = occ.astype(jnp.float32)
    state = filled[:, 0, :, None] * embed[0] + filled[:, 1, :, None] * embed[1] + embed[2]
    mixed = None
    pre = None
    for layer in range(weights.shape[0]):
        conv = depthwise(state.reshape(count, LAT, LAT, -1), kernels[layer])
        mixed = conv.reshape(count, cells, -1).astype(jnp.bfloat16)
        pre = jnp.dot(mixed.reshape(count * cells, -1), weights[layer], preferred_element_type=jnp.float32).reshape(count, cells, -1) + biases[layer]
        state = state + jax.nn.silu(pre)
    logamp = jnp.sum(jnp.tanh(state) * readout, axis=(1, 2))
    return logamp, mixed, pre, state


def silu_slope(value):
    sig = jax.nn.sigmoid(value)
    return sig * (1.0 + value * (1.0 - sig))


def reference(sample_occ, unique_occ, conn_index, hop_sign, gram_owner, embed, kernels, weights, biases, readout):
    def unique_block(group):
        return network(group, embed, kernels, weights, biases, readout)[0]

    unique_logamp = lax.map(unique_block, unique_occ.reshape(-1, U_DEV, 2, SITES)).reshape(-1)

    def sample_block(group):
        logamp, mixed, pre, state = network(group, embed, kernels, weights, biases, readout)
        cotangent = (readout * (1.0 - jnp.tanh(state) ** 2) * silu_slope(pre)).astype(jnp.bfloat16)
        rows = jnp.einsum("bsc,bsd->bcd", mixed.astype(jnp.float32), cotangent.astype(jnp.float32))
        return logamp, rows.astype(jnp.bfloat16).reshape(group.shape[0], -1)

    block = S_DEV * 8
    sample_logamp, jacobian = lax.map(sample_block, sample_occ.reshape(-1, block, 2, SITES))
    sample_logamp = sample_logamp.reshape(-1)
    jacobian = jacobian.reshape(N_S, CH * CH)
    picked = jnp.take(unique_logamp, conn_index, axis=0)
    sign = (2 * hop_sign - 1).astype(jnp.float32)
    hopping = -HOP * jnp.sum(sign * jnp.exp(picked - sample_logamp[:, None]), axis=1)
    filled = sample_occ.astype(jnp.float32)
    onsite = INTER * jnp.sum((filled[:, 0] - 0.5) * (filled[:, 1] - 0.5), axis=1)
    local_energy = hopping + onsite
    shifted = local_energy - jnp.mean(local_energy)
    wide = jacobian.astype(jnp.float32)
    centered = (wide - jnp.mean(wide, axis=0)).astype(jnp.bfloat16)
    force = jnp.dot(shifted, centered.astype(jnp.float32), precision=lax.Precision.HIGHEST) / N_S
    whole = jnp.dot(centered, centered.T, preferred_element_type=jnp.float32) / N_S
    gram = jnp.take(whole.reshape(DEVICES, S_DEV, N_S), gram_owner, axis=0).reshape(N_S, N_S)
    return local_energy, gram, force
```

```python
import jax
import jax.numpy as jnp
from jax import lax
from jax.experimental import pallas as pl
from jax.experimental.pallas import tpu as pltpu
from jax.sharding import PartitionSpec as P

MESH = pl.DeviceIdType.MESH
F32 = jnp.float32
BF16 = jnp.bfloat16
NZ, NY, NX, NK = 8, 4, 4, 2
N_S = 1024
T0 = (((0,), (0,)), ((), ()))
NT = (((1,), (1,)), ((), ()))


def iota(shape, dim):
    return lax.broadcasted_iota(jnp.int32, shape, dim)


def patch_rows(occ_ref, zed_ref, rows):
    sub = iota((rows, 8, 128), 1)
    t = occ_ref[...]
    r = [t if dy == 2 else pltpu.roll(t, (8 * (2 - dy)) % 128, 2) for dy in range(5)]
    first = jnp.where(sub < 2, r[0], jnp.where(sub < 4, r[1], jnp.where(sub < 6, r[2], r[3])))
    second = jnp.where(sub < 2, r[4], jnp.where(sub == 2, 1.0, 0.0))
    zed_ref[:, 0:8, :] = first
    zed_ref[:, 8:16, :] = second


def first_layer(zed_ref, wz_ref, w_ref, b_ref, state_ref, rows):
    many = 4

    def step(i, carry):
        xs = [i * many + k for k in range(many)]
        cols = []
        for x in xs:
            taps = [zed_ref[x + j].astype(BF16) for j in range(5)]
            cols.append(jnp.concatenate(taps + taps, axis=0))
        cols = jnp.concatenate(cols, axis=1)
        both = lax.dot_general(cols, wz_ref[...], T0, preferred_element_type=F32)
        mixed = both[:, :256].astype(BF16)
        pre = jnp.dot(mixed, w_ref[0], preferred_element_type=F32) + b_ref[0:1, :]
        half = 0.5 * pre
        new = both[:, 256:] + (half + half * jnp.tanh(half))
        state_ref[pl.ds(i * many + 2, many)] = new.reshape(many, 16, 8, 256)
        return carry

    lax.fori_loop(0, rows // many, step, 0)


def halo(state_ref, rows, swap):
    for i in (0, 1):
        low = state_ref[rows + i]
        high = state_ref[2 + i]
        if swap:
            low = pltpu.roll(low, 4, 1)
            high = pltpu.roll(high, 4, 1)
        state_ref[i] = low
        state_ref[rows + 2 + i] = high


def convolve(state_ref, kb_ref, x):
    halves = []
    for h in range(2):
        lanes = slice(128 * h, 128 * h + 128)
        acc = None
        for dx in range(5):
            row = state_ref[x + dx, :, :, lanes]
            for dy in range(5):
                s = (dy - 2) % 16
                moved = row if s == 0 else jnp.concatenate([row[s:], row[:s]], axis=0)
                term = moved * kb_ref[dx * 5 + dy, :, lanes][None]
                acc = term if acc is None else acc + term
        halves.append(acc.reshape(128, 128))
    return jnp.concatenate(halves, axis=1)


def second_layer(state_ref, kb_ref, mix_ref, w_ref, b_ref, rows, keep_mixed=None, keep_rest=None):
    def finish(x, total):
        pre = jnp.dot(mix_ref[lax.rem(x, 2)], w_ref[1], preferred_element_type=F32) + b_ref[1:2, :]
        half = 0.5 * pre
        th_half = jnp.tanh(half)
        out = jnp.tanh(state_ref[x + 2].reshape(128, 256) + (half + half * th_half))
        if keep_rest is not None:
            keep_rest(x, pre, th_half, out)
        return total + jnp.sum(out.reshape(16, 8, 256), axis=0)

    def make(x):
        mixed = convolve(state_ref, kb_ref, x)
        mix_ref[lax.rem(x, 2)] = mixed.astype(BF16)
        if keep_mixed is not None:
            keep_mixed(x, mixed)

    make(jnp.int32(0))

    def step(x, total):
        total = finish(x - 1, total)
        make(x)
        return total

    total = lax.fori_loop(1, rows, step, jnp.zeros((8, 256), F32))
    return finish(jnp.int32(rows - 1), total)


class Wire:
    def __init__(self, send, recv):
        e, x = lax.axis_index("eval"), lax.axis_index("blk")
        self.at = {
            "z": lax.div(e, NY * NK),
            "y": lax.rem(lax.div(e, NK), NY),
            "k": lax.rem(e, NK),
            "x": x,
        }
        self.size = {"z": NZ, "y": NY, "k": NK, "x": NX}
        self.send, self.recv, self.used = send, recv, 0

    def peer(self, axis, off):
        return lax.rem(self.at[axis] + off, self.size[axis])

    def device(self, axis, place):
        at = {**self.at, axis: place}
        return ((at["z"] * NY + at["y"]) * NK + at["k"], at["x"])

    def barrier(self):
        sem = pltpu.get_barrier_semaphore()
        count = 0
        for axis, size in self.size.items():
            for off in range(1, size):
                pl.semaphore_signal(
                    sem, inc=1, device_id=self.device(axis, self.peer(axis, off)), device_id_type=MESH
                )
                count += 1
        pl.semaphore_wait(sem, count)

    def start(self, axis, src, dst):
        copies = []
        for off in range(1, self.size[axis]):
            place = self.peer(axis, off)
            copy = pltpu.make_async_remote_copy(
                src_ref=src(place),
                dst_ref=dst,
                send_sem=self.send.at[self.used],
                recv_sem=self.recv.at[self.used],
                device_id=self.device(axis, place),
                device_id_type=MESH,
            )
            copy.start()
            self.used += 1
            copies.append(copy)
        return copies


def wait(*groups):
    for group in groups:
        for copy in group:
            copy.wait()


def jacobian(mixf_ref, cotf_ref, jf_ref, send_refs):
    for s in range(4):
        rows = pl.ds(s, 256, stride=4)
        left = jnp.concatenate([mixf_ref[h, rows, :] for h in range(2)], axis=1).astype(BF16)
        right = jnp.concatenate([cotf_ref[h, rows, :] for h in range(2)], axis=1).astype(BF16)
        out = lax.dot_general(left, right, T0, preferred_element_type=F32)
        for h in range(2):
            jf_ref[h, pl.ds(s, 256, stride=8), :] = out[:, 128 * h : 128 * h + 128]
    low = iota((NY, NX, 8, 128), 2) < 4

    def step(z, carry):
        for h in range(2):
            t = jf_ref[h, pl.ds(z * 256, 256), :].reshape(NY, NK, NX, 8, 128)
            send_refs[h][z] = jnp.where(low, t[:, 0], pltpu.roll(t[:, 1], 4, 2)).astype(BF16)
        return carry

    lax.fori_loop(0, NZ, step, 0)


def center(full_refs, xc_ref, xn_ref):
    for h in range(2):

        def add(z, total):
            return total + jnp.sum(full_refs[h][z].reshape(32, 8, 128).astype(F32), axis=0)

        total = lax.fori_loop(0, NZ, add, jnp.zeros((8, 128), F32))
        means = [jnp.sum(total[4 * k : 4 * k + 4], axis=0, keepdims=True) / N_S for k in range(2)]
        mean = jnp.where(iota((8, 128), 0) < 4, means[0], means[1])

        def step(z, carry):
            t = full_refs[h][z].reshape(32, 8, 128).astype(F32) - mean[None]
            t = t.astype(BF16).astype(F32)
            xc_ref[h, pl.ds(z * 32, 32)] = t
            t = t.reshape(16, 2, 8, 128)
            low = iota((16, 8, 128), 1) < 4
            one = jnp.where(low, t[:, 0], pltpu.roll(t[:, 1], 4, 1))
            two = jnp.where(low, pltpu.roll(t[:, 0], 4, 1), t[:, 1])
            xn_ref[0, pl.ds(z * 128, 128), 128 * h : 128 * h + 128] = one.reshape(128, 128).astype(BF16)
            xn_ref[1, pl.ds(z * 128, 128), 128 * h : 128 * h + 128] = two.reshape(128, 128).astype(BF16)
            return carry

        lax.fori_loop(0, NZ, step, 0)


def gram_rows(owner_ref, core, xc_ref, left_ref):
    low = iota((8, 128), 0) < 4

    def step(q, carry):
        target = lax.div(q, NX) * (NK * NX) + core * NX + lax.rem(q, NX)
        own = owner_ref[target]
        for h in range(2):
            t = xc_ref[h, own]
            r = pltpu.roll(t, 4, 0)
            left_ref[0, q, :, 128 * h : 128 * h + 128] = jnp.where(low, t, r)
            left_ref[1, q, :, 128 * h : 128 * h + 128] = jnp.where(low, r, t)
        return carry

    lax.fori_loop(0, NZ * NY * NX, step, 0)


def gram_part(left_ref, xn_ref, ga_ref, gb_ref):
    low = lax.rem(lax.div(iota((128, 512), 0), 4), 2) == 0

    def step(z, carry):
        total = None
        for k in range(2):
            rows = left_ref[k, pl.ds(z * 16, 16)].reshape(128, 256).astype(BF16)
            part = lax.dot_general(rows, xn_ref[k], NT, preferred_element_type=F32)
            total = part if total is None else total + part
        out = (jnp.where(low, total[:, :512], total[:, 512:]) * (1.0 / N_S)).astype(BF16)
        ga_ref[z] = out[:, :256].reshape(NY, NX, 8, 256)
        gb_ref[z] = out[:, 256:].reshape(NY, NX, 8, 256)
        return carry

    lax.fori_loop(0, NZ, step, 0)


def add_outer(own, got_ref, out_ref, at, size):
    def step(z, carry):
        total = own(z).astype(F32)
        for off in range(1, size):
            total = total + got_ref[lax.rem(at + off, size), z].astype(F32)
        out_ref[z] = total.astype(BF16)
        return carry

    lax.fori_loop(0, NZ, step, 0)


def add_inner(own, got_ref, at, size):
    total = own.astype(F32)
    for off in range(1, size):
        total = total + got_ref[lax.rem(at + off, size)].astype(F32)
    return total


def kernel(
    owner_ref, occ_s_ref, occ_u_ref, info_ref, wz_ref, w_ref, b_ref, k_ref, ro_ref,
    energy_ref, gram_ref, force_ref,
    zs, zu, ss, su, kb, mix, mixf, cotf, jf, xc, xn, left, uv, dense, part,
    a0, a1, a2, b0, b1, b2, fa, fb, ag,
    ga, gb, ra1, rb1, ga2, gb2, ra2, rb2, ga3, gb3, ra3, rb3,
    arz, ary, arx, ark,
    send, recv,
):
    wire = Wire(send, recv)
    mz, my, mk, mx = (wire.at[a] for a in "zykx")
    wire.barrier()
    for t in range(25):
        kb[t] = jnp.broadcast_to(k_ref[t : t + 1, :], (8, 256))

    patch_rows(occ_s_ref, zs, 12)
    first_layer(zs, wz_ref, w_ref, b_ref, ss, 8)
    halo(ss, 8, True)

    def keep_mixed(x, mixed):
        for h in range(2):
            mixf[h, pl.ds(x * 128, 128), :] = mixed[:, 128 * h : 128 * h + 128].astype(BF16).astype(F32)

    def keep_cot(x, pre, th, out):
        g = 0.5 + 0.5 * th
        cot = ro_ref[...] * (1.0 - out * out) * (g * (1.0 + pre * (1.0 - g)))
        for h in range(2):
            cotf[h, pl.ds(x * 128, 128), :] = cot[:, 128 * h : 128 * h + 128].astype(BF16).astype(F32)

    sums = second_layer(ss, kb, mix, w_ref, b_ref, 8, keep_mixed, keep_cot)
    amp = jnp.broadcast_to(jnp.sum(sums * ro_ref[...], axis=1, keepdims=True), (8, 128))
    amp = amp + pltpu.roll(amp, 4, 0)
    jacobian(mixf, cotf, jf, (a0, b0))

    go_a = wire.start("z", lambda p: a0.at[p], a1.at[mz])
    go_b = wire.start("x", lambda p: b0.at[:, :, p], b1.at[:, :, mx])
    sub, lane = iota((8, 128), 0), iota((8, 128), 1)
    amp = jnp.sum(jnp.where(sub == lax.rem(lane, 4), amp, 0.0), axis=0, keepdims=True)
    ag[mz, my, mk, mx] = jnp.where(sub == 2, amp, info_ref[...])
    go_i = wire.start("z", lambda p: ag.at[mz, my, mk, mx], ag.at[mz, my, mk, mx])
    a1[mz] = a0[mz]
    b1[:, :, mx] = b0[:, :, mx]

    def unique(g):
        patch_rows(occ_u_ref.at[g], zu, 20)
        first_layer(zu, wz_ref, w_ref, b_ref, su, 16)
        halo(su, 16, False)

    def unique_end(g):
        sums = second_layer(su, kb, mix, w_ref, b_ref, 16)
        uv[8 * g : 8 * g + 8, :] = jnp.broadcast_to(
            jnp.sum(sums * ro_ref[...], axis=1, keepdims=True), (8, 128)
        )

    unique(0)
    unique_end(0)
    wait(go_a, go_b, go_i)

    go_a = wire.start("y", lambda p: a1.at[:, p], a2.at[:, my])
    go_b = wire.start("y", lambda p: b1.at[:, p], b2.at[:, my])
    go_i = wire.start("y", lambda p: ag.at[:, my, mk, mx], ag.at[:, my, mk, mx])
    a2[:, my] = a1[:, my]
    b2[:, my] = b1[:, my]
    unique(1)
    unique_end(1)
    wait(go_a, go_b, go_i)

    go_a = wire.start("x", lambda p: a2.at[:, :, p], fa.at[:, :, mk, mx])
    go_b = wire.start("z", lambda p: b2.at[p], fb.at[mz, :, mk])
    go_i = wire.start("x", lambda p: ag.at[:, :, mk, mx], ag.at[:, :, mk, mx])
    fa[:, :, mk, mx] = a2[:, :, mx]
    fb[mz, :, mk] = b2[mz]
    unique(2)
    unique_end(2)
    wait(go_a, go_b, go_i)

    go_a = wire.start("k", lambda p: fa.at[:, :, mk], fa.at[:, :, mk])
    go_b = wire.start("k", lambda p: fb.at[:, :, mk], fb.at[:, :, mk])
    go_i = wire.start("k", lambda p: ag.at[:, :, mk], ag.at[:, :, mk])
    unique(3)
    wait(go_a, go_b, go_i)

    center((fa, fb), xc, xn)
    gram_rows(owner_ref, mk, xc, left)
    gram_part(left, xn, ga, gb)

    go_a = wire.start("x", lambda p: ga.at[:, :, p], ra1.at[mx])
    go_b = wire.start("y", lambda p: gb.at[:, p], rb1.at[my])
    unique_end(3)

    flat = ag.reshape(2048, 128)
    mine = ((mz * NY + my) * NK + mk) * NX + mx
    for r in range(8):
        for row in range(4):
            dense[row, pl.ds(32 * r, 32), :] = flat[pl.ds(256 * r + row, 32, stride=8), :]
    place = iota((32, 128), 0) == lax.div(iota((32, 128), 1), 4)
    hop, site = [], []
    for r in range(8):
        rows = pl.ds(32 * r, 32)
        local = dense[0, rows, :] - (32 * mine).astype(F32)
        pick = jnp.zeros((32, 128), F32)
        for u in range(32):
            pick = jnp.where(local == u, uv[u : u + 1, :], pick)
        known = jnp.logical_and(local > -0.5, local < 31.5)
        value = jnp.where(known, pick - dense[2, rows, :], 0.0)
        value = jnp.where(known, dense[1, rows, :] * jnp.exp(value), 0.0)
        for shift in (4, 8, 16, 32, 64):
            value = value + pltpu.roll(value, shift, 1)
        hop.append(jnp.sum(jnp.where(place, value, 0.0), axis=0, keepdims=True))
        site.append(jnp.sum(jnp.where(place, dense[3, rows, :], 0.0), axis=0, keepdims=True))
    part[0] = jnp.concatenate(hop, axis=0)
    go_e = wire.start("z", lambda p: part.at[0], arz.at[mz])

    wait(go_a, go_b)
    add_outer(lambda z: ga[z, :, mx], ra1, ga2, mx, NX)
    add_outer(lambda z: gb[z, my], rb1, gb2, my, NY)
    go_a = wire.start("y", lambda p: ga2.at[:, p], ra2.at[my])
    go_b = wire.start("x", lambda p: gb2.at[:, p], rb2.at[mx])
    wait(go_e)
    part[1] = add_inner(part[0], arz, mz, NZ)
    go_e = wire.start("y", lambda p: part.at[1], ary.at[my])
    wait(go_a, go_b)
    ga3[...] = add_inner(ga2[:, my], ra2, my, NY).astype(BF16)
    gb3[...] = add_inner(gb2[:, mx], rb2, mx, NX).astype(BF16)
    go_a = wire.start("z", lambda p: ga3.at[p], ra3.at[mz])
    go_b = wire.start("z", lambda p: gb3.at[p], rb3.at[mz])
    wait(go_e)
    part[2] = add_inner(part[1], ary, my, NY)
    go_e = wire.start("x", lambda p: part.at[2], arx.at[mx])
    wait(go_e)
    part[3] = add_inner(part[2], arx, mx, NX)
    go_e = wire.start("k", lambda p: part.at[3], ark.at[mk])
    wait(go_e)
    hopping = add_inner(part[3], ark, mk, NK)
    energy = jnp.concatenate(site, axis=0) - hopping
    energy_ref[...] = energy
    shifted = energy - jnp.sum(energy) / N_S
    high = shifted.astype(BF16)
    rest = shifted - high.astype(F32)
    middle = rest.astype(BF16)
    low = (rest - middle.astype(F32)).astype(BF16)
    three = jnp.concatenate([high, middle, low], axis=0)
    force = jnp.zeros((8, 256), F32)
    for r in range(8):
        out = jnp.dot(three, xn[mk, pl.ds(128 * r, 128), :], preferred_element_type=F32)
        out = out[0:8] + out[8:16] + out[16:24]
        force = force + jnp.where(iota((8, 256), 0) == r, out, 0.0)
    force_ref[...] = jnp.sum(force, axis=0, keepdims=True) / N_S

    wait(go_a, go_b)
    one = add_inner(ga3[mz], ra3, mz, NZ)
    two = add_inner(gb3[mz], rb3, mz, NZ)
    for h in range(2):
        gram_ref[:, 512 * h : 512 * h + 256] = one[4 * h : 4 * h + 4]
        gram_ref[:, 512 * h + 256 : 512 * h + 512] = two[4 * h : 4 * h + 4]


def tap_weights(embed, kernels):
    taps = (kernels[0].reshape(5, 5, 1, 256) * embed[:2][None, None]).reshape(5, 10, 256)
    left = jnp.pad(taps, ((0, 0), (0, 6), (0, 0)))
    left = left.at[0, 10].set(embed[2] * jnp.sum(kernels[0], axis=0))
    right = jnp.zeros((5, 16, 256), F32).at[2, 4:6].set(embed[:2]).at[0, 10].set(embed[2])
    base = jnp.concatenate([left, right], axis=2).reshape(80, 512)
    high = lax.reduce_precision(base, 8, 7)
    return jnp.concatenate([high.astype(BF16), (base - high).astype(BF16)], axis=0)


def body(sample_occ, unique_occ, conn_index, hop_sign, gram_owner, embed, kernels, weights, biases, readout):
    occ_u = unique_occ.astype(F32).reshape(4, 8, 2, 16, 16).transpose(0, 3, 2, 4, 1).reshape(4, 16, 2, 128)
    occ_u = jnp.tile(jnp.concatenate([occ_u[:, 14:], occ_u, occ_u[:, :2]], axis=1), (1, 1, 4, 1))
    filled = sample_occ.astype(F32)
    occ_s = filled.reshape(4, 2, 16, 16).transpose(2, 1, 3, 0)
    occ_s = jnp.concatenate([occ_s[14:], occ_s, occ_s[:2]], axis=0)
    occ_s = jnp.stack([occ_s[:12], occ_s[8:]], axis=3).reshape(12, 2, 128)
    occ_s = jnp.tile(occ_s, (1, 4, 1))
    onsite = 4.0 * jnp.sum((filled[:, 0] - 0.5) * (filled[:, 1] - 0.5), axis=1)
    index = conn_index.astype(F32).T.reshape(1, 128)
    sign = (2 * hop_sign - 1).astype(F32).T.reshape(1, 128)
    info = jnp.concatenate(
        [index, sign, jnp.zeros((1, 128), F32), jnp.tile(onsite, 32)[None], jnp.zeros((4, 128), F32)], axis=0
    )
    vmem = pl.BlockSpec(memory_space=pltpu.VMEM)
    smem = pl.BlockSpec(memory_space=pltpu.SMEM)
    grid = (NZ, NY, NX, 8, 128)
    energy, gram, force = pl.pallas_call(
        kernel,
        out_shape=(
            jax.ShapeDtypeStruct((8, 128), F32),
            jax.ShapeDtypeStruct((4, N_S), F32),
            jax.ShapeDtypeStruct((1, 256), F32),
        ),
        in_specs=[smem] + [vmem] * 8,
        out_specs=(vmem, vmem, vmem),
        scratch_shapes=[
            pltpu.VMEM((12, 16, 128), F32),
            pltpu.VMEM((20, 16, 128), F32),
            pltpu.VMEM((12, 16, 8, 256), F32),
            pltpu.VMEM((20, 16, 8, 256), F32),
            pltpu.VMEM((25, 8, 256), F32),
            pltpu.VMEM((2, 128, 256), BF16),
            pltpu.VMEM((2, 1024, 128), F32),
            pltpu.VMEM((2, 1024, 128), F32),
            pltpu.VMEM((2, 2048, 128), F32),
            pltpu.VMEM((2, 256, 8, 128), F32),
            pltpu.VMEM((2, 1024, 256), BF16),
            pltpu.VMEM((2, 128, 8, 256), F32),
            pltpu.VMEM((32, 128), F32),
            pltpu.VMEM((4, 256, 128), F32),
            pltpu.VMEM((4, 8, 128), F32),
        ]
        + [pltpu.VMEM(grid, BF16)] * 6
        + [pltpu.VMEM((NZ, NY, NK, NX, 8, 128), BF16)] * 2
        + [pltpu.VMEM((NZ, NY, NK, NX, 8, 128), F32)]
        + [pltpu.VMEM((NZ, NY, NX, 8, 256), BF16)] * 2
        + [pltpu.VMEM((4, NZ, 4, 8, 256), BF16)] * 2
        + [pltpu.VMEM((NZ, 4, 8, 256), BF16)] * 2
        + [pltpu.VMEM((4, NZ, 8, 256), BF16)] * 2
        + [pltpu.VMEM((NZ, 8, 256), BF16)] * 4
        + [pltpu.VMEM((n, 8, 128), F32) for n in (NZ, NY, NX, NK)]
        + [pltpu.SemaphoreType.DMA((96,)), pltpu.SemaphoreType.DMA((96,))],
        compiler_params=pltpu.CompilerParams(
            collective_id=0, has_side_effects=True, vmem_limit_bytes=48 << 20
        ),
        name="local_energy_gram",
    )(
        gram_owner, occ_s, occ_u, info, tap_weights(embed, kernels), weights, biases, kernels[1],
        readout.reshape(1, 256),
    )
    mine = lax.axis_index(("eval", "blk"))
    return lax.dynamic_slice_in_dim(energy.reshape(N_S), 4 * mine, 4), gram, force.reshape(256)


def solution(mesh):
    both = ("eval", "blk")
    return jax.shard_map(
        body,
        mesh=mesh,
        in_specs=(P(both), P(both), P(both), P(both), P(), P(), P(), P(), P(), P()),
        out_specs=(P(both), P(both), P(both)),
        check_vma=False,
    )
```

```python
import jax
import jax.numpy as jnp
from jax import lax
from jax.experimental import pallas as pl
from jax.experimental.pallas import tpu as pltpu
from jax.sharding import PartitionSpec as P

MESH = pl.DeviceIdType.MESH
F32 = jnp.float32
BF16 = jnp.bfloat16
NZ, NY, NX, NK = 8, 4, 4, 2
N_S = 1024
T0 = (((0,), (0,)), ((), ()))
NT = (((1,), (1,)), ((), ()))


def iota(shape, dim):
    return lax.broadcasted_iota(jnp.int32, shape, dim)


def spread_table(spread_ref):
    site, lane = iota((256, 128), 0), iota((256, 128), 1)
    same = lax.rem(site, 16) == lax.div(lane, 8)
    for c in range(8):
        hit = jnp.logical_and(same, lax.rem(lane, 8) == c)
        spread_ref[c] = jnp.where(hit, 1.0, 0.0).astype(BF16)


def occupied(occ_ref, first, spread_ref, rows, split):
    total = None
    sub, lane = iota((1, 8, 256), 1), iota((rows, 8, 256), 2)
    for c in range(8):
        o = occ_ref[first + (c % 4 if split else c)].astype(F32)
        o = jnp.where(lax.rem(sub, 2) == 0, o[0:1, :][None], o[1:2, :][None])
        row = lax.rem(iota((rows, 8, 256), 0) + (14 + (8 * (c // 4) if split else 0)), 16)
        o = jnp.where(lax.div(lane, 16) == row, o, 0.0).reshape(rows * 8, 256).astype(BF16)
        part = jnp.dot(o, spread_ref[c], preferred_element_type=F32)
        total = part if total is None else total + part
    return total.reshape(rows, 8, 128)


def patch_rows(t, zed_ref, rows):
    sub = iota((rows, 8, 128), 1)
    r = [t if dy == 2 else pltpu.roll(t, (8 * (2 - dy)) % 128, 2) for dy in range(5)]
    first = jnp.where(sub < 2, r[0], jnp.where(sub < 4, r[1], jnp.where(sub < 6, r[2], r[3])))
    second = jnp.where(sub < 2, r[4], jnp.where(sub == 2, 1.0, 0.0))
    zed_ref[:, 0:8, :] = first
    zed_ref[:, 8:16, :] = second


def tap_weights(embed_ref, k_ref, wz_ref):
    sub = iota((8, 256), 0)
    spin = jnp.where(lax.rem(sub, 2) == 0, embed_ref[0:1, :], embed_ref[1:2, :])
    const = embed_ref[2:3, :] * jnp.sum(k_ref[0], axis=0, keepdims=True)
    for dx in range(5):
        k = [k_ref[0, dx * 5 + dy : dx * 5 + dy + 1, :] for dy in range(5)]
        top = jnp.where(sub < 2, k[0], jnp.where(sub < 4, k[1], jnp.where(sub < 6, k[2], k[3]))) * spin
        low = jnp.where(sub < 2, k[4] * spin, jnp.where(sub == 2, const, 0.0) if dx == 0 else 0.0)
        own = jnp.where(lax.div(sub, 2) == 2, spin, 0.0) if dx == 2 else jnp.zeros((8, 256), F32)
        one = jnp.where(sub == 2, embed_ref[2:3, :], 0.0) if dx == 0 else jnp.zeros((8, 256), F32)
        base = jnp.concatenate(
            [jnp.concatenate([top, low], axis=0), jnp.concatenate([own, one], axis=0)], axis=1
        )
        high = base.astype(BF16)
        wz_ref[16 * dx : 16 * dx + 16, :] = high
        wz_ref[80 + 16 * dx : 96 + 16 * dx, :] = (base - high.astype(F32)).astype(BF16)


def first_layer(zed_ref, wz_ref, w_ref, b_ref, state_ref, rows):
    many = 4

    def step(i, carry):
        xs = [i * many + k for k in range(many)]
        cols = []
        for x in xs:
            taps = [zed_ref[x + j].astype(BF16) for j in range(5)]
            cols.append(jnp.concatenate(taps + taps, axis=0))
        cols = jnp.concatenate(cols, axis=1)
        both = lax.dot_general(cols, wz_ref[...], T0, preferred_element_type=F32)
        mixed = both[:, :256].astype(BF16)
        pre = jnp.dot(mixed, w_ref[0], preferred_element_type=F32) + b_ref[0:1, :]
        half = 0.5 * pre
        new = both[:, 256:] + (half + half * jnp.tanh(half))
        state_ref[pl.ds(i * many + 2, many)] = new.reshape(many, 16, 8, 256)
        return carry

    lax.fori_loop(0, rows // many, step, 0)


def halo(state_ref, rows, swap):
    for i in (0, 1):
        low = state_ref[rows + i]
        high = state_ref[2 + i]
        if swap:
            low = pltpu.roll(low, 4, 1)
            high = pltpu.roll(high, 4, 1)
        state_ref[i] = low
        state_ref[rows + 2 + i] = high


def convolve(state_ref, kb_ref, x):
    halves = []
    for h in range(2):
        lanes = slice(128 * h, 128 * h + 128)
        acc = None
        for dx in range(5):
            row = state_ref[x + dx, :, :, lanes]
            for dy in range(5):
                s = (dy - 2) % 16
                moved = row if s == 0 else jnp.concatenate([row[s:], row[:s]], axis=0)
                term = moved * kb_ref[dx * 5 + dy, :, lanes][None]
                acc = term if acc is None else acc + term
        halves.append(acc.reshape(128, 128))
    return jnp.concatenate(halves, axis=1)


class SecondLayer:
    def __init__(self, state_ref, kb_ref, mix_ref, w_ref, b_ref, total_ref, rows, keep_mixed=None, keep_rest=None):
        self.state, self.kb, self.mix, self.w, self.b = state_ref, kb_ref, mix_ref, w_ref, b_ref
        self.total, self.rows, self.keep_mixed, self.keep_rest = total_ref, rows, keep_mixed, keep_rest

    def finish(self, x, total):
        pre = jnp.dot(self.mix[lax.rem(x, 2)], self.w[1], preferred_element_type=F32) + self.b[1:2, :]
        half = 0.5 * pre
        th_half = jnp.tanh(half)
        out = jnp.tanh(self.state[x + 2].reshape(128, 256) + (half + half * th_half))
        if self.keep_rest is not None:
            self.keep_rest(x, pre, th_half, out)
        return total + jnp.sum(out.reshape(16, 8, 256), axis=0)

    def make(self, x):
        mixed = convolve(self.state, self.kb, x)
        self.mix[lax.rem(x, 2)] = mixed.astype(BF16)
        if self.keep_mixed is not None:
            self.keep_mixed(x, mixed)

    def part(self, low, high):
        if low == 0:
            self.make(jnp.int32(0))
            self.total[...] = jnp.zeros((8, 256), F32)

        def step(x, total):
            total = self.finish(x - 1, total)
            self.make(x)
            return total

        total = lax.fori_loop(max(low, 1), high, step, self.total[...])
        self.total[...] = self.finish(jnp.int32(high - 1), total) if high == self.rows else total


class Wire:
    def __init__(self, send, recv):
        e, x = lax.axis_index("eval"), lax.axis_index("blk")
        self.at = {
            "z": lax.div(e, NY * NK),
            "y": lax.rem(lax.div(e, NK), NY),
            "k": lax.rem(e, NK),
            "x": x,
        }
        self.size = {"z": NZ, "y": NY, "k": NK, "x": NX}
        self.send, self.recv, self.used = send, recv, 0

    def peer(self, axis, off):
        return lax.rem(self.at[axis] + off, self.size[axis])

    def device(self, axis, place):
        at = {**self.at, axis: place}
        return ((at["z"] * NY + at["y"]) * NK + at["k"], at["x"])

    def greet(self):
        sem = pltpu.get_barrier_semaphore()
        count = 0
        for axis, size in self.size.items():
            for off in range(1, size):
                pl.semaphore_signal(
                    sem, inc=1, device_id=self.device(axis, self.peer(axis, off)), device_id_type=MESH
                )
                count += 1
        return sem, count

    def start(self, axis, src, dst):
        copies = []
        for off in range(1, self.size[axis]):
            place = self.peer(axis, off)
            copy = pltpu.make_async_remote_copy(
                src_ref=src(place),
                dst_ref=dst,
                send_sem=self.send.at[self.used],
                recv_sem=self.recv.at[self.used],
                device_id=self.device(axis, place),
                device_id_type=MESH,
            )
            copy.start()
            self.used += 1
            copies.append(copy)
        return copies


def wait(*groups):
    for group in groups:
        for copy in group:
            copy.wait()


def jacobian(mixf_ref, cotf_ref, jf_ref, send_refs):
    for s in range(4):
        rows = pl.ds(s, 256, stride=4)
        left = jnp.concatenate([mixf_ref[h, rows, :] for h in range(2)], axis=1).astype(BF16)
        right = jnp.concatenate([cotf_ref[h, rows, :] for h in range(2)], axis=1).astype(BF16)
        out = lax.dot_general(left, right, T0, preferred_element_type=F32)
        for h in range(2):
            jf_ref[h, pl.ds(s, 256, stride=8), :] = out[:, 128 * h : 128 * h + 128]
    low = iota((NY, NX, 8, 128), 2) < 4

    def step(z, carry):
        for h in range(2):
            t = jf_ref[h, pl.ds(z * 256, 256), :].reshape(NY, NK, NX, 8, 128)
            send_refs[h][z] = jnp.where(low, t[:, 0], pltpu.roll(t[:, 1], 4, 2)).astype(BF16)
        return carry

    lax.fori_loop(0, NZ, step, 0)


def center(full_refs, xc_ref, xn_ref, xt_ref):
    for h in range(2):

        def add(z, total):
            return total + jnp.sum(full_refs[h][z].reshape(32, 8, 128).astype(F32), axis=0)

        total = lax.fori_loop(0, NZ, add, jnp.zeros((8, 128), F32))
        means = [jnp.sum(total[4 * k : 4 * k + 4], axis=0, keepdims=True) / N_S for k in range(2)]
        mean = jnp.where(iota((8, 128), 0) < 4, means[0], means[1])

        def step(z, carry):
            t = full_refs[h][z].reshape(32, 8, 128).astype(F32) - mean[None]
            t = t.astype(BF16).astype(F32)
            xc_ref[h, pl.ds(z * 32, 32)] = t
            t = t.reshape(16, 2, 8, 128)
            low = iota((16, 8, 128), 1) < 4
            one = jnp.where(low, t[:, 0], pltpu.roll(t[:, 1], 4, 1))
            two = jnp.where(low, pltpu.roll(t[:, 0], 4, 1), t[:, 1])
            for k, v in enumerate((one, two)):
                v = v.reshape(128, 128)
                xn_ref[k, pl.ds(z * 128, 128), 128 * h : 128 * h + 128] = v.astype(BF16)
                xt_ref[k, z, 128 * h : 128 * h + 128, :] = v.T.astype(BF16)
            return carry

        lax.fori_loop(0, NZ, step, 0)


def gram_rows(owner_ref, core, xc_ref, left_ref):
    low = iota((8, 128), 0) < 4

    def step(i, carry):
        for j in range(16):
            q = i * 16 + j
            own = owner_ref[i * (2 * NK * NX * 2) + (j // NX) * (NK * NX) + core * NX + j % NX]
            for h in range(2):
                t = xc_ref[h, own]
                r = pltpu.roll(t, 4, 0)
                left_ref[0, q, :, 128 * h : 128 * h + 128] = jnp.where(low, t, r)
                left_ref[1, q, :, 128 * h : 128 * h + 128] = jnp.where(low, r, t)
        return carry

    lax.fori_loop(0, NZ, step, 0)


def gram_part(left_ref, xt_ref, ga_ref, gb_ref):
    low = lax.rem(lax.div(iota((256, 256), 0), 4), 2) == 0

    def step(i, carry):
        rows = [left_ref[k, pl.ds(i * 32, 32)].reshape(256, 256).astype(BF16) for k in range(2)]

        def columns(c):
            out = None
            for k in range(2):
                right = jnp.concatenate([xt_ref[k, 2 * c], xt_ref[k, 2 * c + 1]], axis=1)
                part = jnp.dot(rows[k], right, preferred_element_type=F32)
                out = part if out is None else out + part
            return out

        for c, ref in enumerate((ga_ref, gb_ref)):
            out = jnp.where(low, columns(c), columns(c + 2)) * (1.0 / N_S)
            ref[pl.ds(2 * i, 2)] = out.astype(BF16).reshape(2, NY, NX, 8, 256)
        return carry

    lax.fori_loop(0, NZ // 2, step, 0)


def add_outer(own, got_ref, out_ref, at, size):
    def step(z, carry):
        total = own(z).astype(F32)
        for off in range(1, size):
            total = total + got_ref[lax.rem(at + off, size), z].astype(F32)
        out_ref[z] = total.astype(BF16)
        return carry

    lax.fori_loop(0, NZ, step, 0)


def add_inner(own, got_ref, at, size):
    total = own.astype(F32)
    for off in range(1, size):
        total = total + got_ref[lax.rem(at + off, size)].astype(F32)
    return total


def own_info(index_ref, sign_ref, occ_ref, amp):
    sub, lane = iota((4, 128), 0), iota((4, 128), 1)
    pick = jnp.where(iota((32, 128), 0) == lax.div(iota((32, 128), 1), 4), 1.0, 0.0).astype(BF16)
    mine = sub == lax.rem(lane, 4)

    def row(v):
        v = jnp.dot(v.astype(F32).astype(BF16), pick, preferred_element_type=F32)
        return jnp.sum(jnp.where(mine, v, 0.0), axis=0, keepdims=True)

    index = index_ref[...]
    rows = [row(lax.shift_right_logical(index, 5)), row(jnp.bitwise_and(index, 31)), row(2 * sign_ref[...] - 1)]
    whole = jnp.sum(jnp.where(iota((8, 128), 0) == lax.rem(iota((8, 128), 1), 4), amp, 0.0), axis=0, keepdims=True)
    for _ in range(3):
        part = whole.astype(BF16).astype(F32)
        rows.append(part)
        whole = whole - part
    site = jnp.zeros((1, 128), F32)
    for i in range(4):
        o = occ_ref[i].astype(F32) - 0.5
        value = 4.0 * jnp.sum(o[0:1, :] * o[1:2, :], axis=1, keepdims=True)
        site = jnp.where(lax.rem(iota((1, 128), 1), 4) == i, value, site)
    rows += [site, jnp.zeros((1, 128), F32)]
    return jnp.concatenate(rows, axis=0).astype(BF16)


def kernel(
    owner_ref, occ_s_ref, occ_u_ref, index_ref, sign_ref, embed_ref, k_ref, w_ref, b_ref, ro_ref,
    energy_ref, gram_ref, force_ref,
    spread, wz, zs, zu, ss, su, kb, mix, sums, mixf, cotf, jf, xc, xn, xt, left, uv, dense, part,
    a0, a1, a2, b0, b1, b2, fa, fb, ag, agf,
    ga, gb, ra1, rb1, ga2, gb2, ra2, rb2, ga3, gb3, ra3, rb3,
    arz, ary, arx, ark,
    send, recv,
):
    wire = Wire(send, recv)
    mz, my, mk, mx = (wire.at[a] for a in "zykx")
    entry, count = wire.greet()
    for t in range(25):
        kb[t] = jnp.broadcast_to(k_ref[1, t : t + 1, :], (8, 256))
    spread_table(spread)
    tap_weights(embed_ref, k_ref, wz)

    patch_rows(occupied(occ_s_ref, 0, spread, 12, True), zs, 12)
    first_layer(zs, wz, w_ref, b_ref, ss, 8)
    halo(ss, 8, True)

    def keep_mixed(x, mixed):
        for h in range(2):
            mixf[h, pl.ds(x * 128, 128), :] = mixed[:, 128 * h : 128 * h + 128].astype(BF16).astype(F32)

    def keep_cot(x, pre, th, out):
        g = 0.5 + 0.5 * th
        cot = ro_ref[...] * (1.0 - out * out) * (g * (1.0 + pre * (1.0 - g)))
        for h in range(2):
            cotf[h, pl.ds(x * 128, 128), :] = cot[:, 128 * h : 128 * h + 128].astype(BF16).astype(F32)

    SecondLayer(ss, kb, mix, w_ref, b_ref, sums, 8, keep_mixed, keep_cot).part(0, 8)
    jacobian(mixf, cotf, jf, (a0, b0))
    pl.semaphore_wait(entry, count)

    go_a = wire.start("z", lambda p: a0.at[p], a1.at[mz])
    go_b = wire.start("y", lambda p: b0.at[:, p], b1.at[:, my])
    amp = jnp.broadcast_to(jnp.sum(sums[...] * ro_ref[...], axis=1, keepdims=True), (8, 128))
    amp = amp + pltpu.roll(amp, 4, 0)
    ag[mz, my, mk, mx] = own_info(index_ref, sign_ref, occ_s_ref, amp)
    go_i = wire.start("z", lambda p: ag.at[mz, my, mk, mx], ag.at[mz, my, mk, mx])
    a1[mz] = a0[mz]
    b1[:, my] = b0[:, my]

    layer = SecondLayer(su, kb, mix, w_ref, b_ref, sums, 16)

    def unique():
        for g in range(4):
            patch_rows(occupied(occ_u_ref, 8 * g, spread, 20, False), zu, 20)
            first_layer(zu, wz, w_ref, b_ref, su, 16)
            halo(su, 16, False)
            yield
            for x in range(0, 16, 4):
                layer.part(x, x + 4)
                if x == 12:
                    uv[8 * g : 8 * g + 8, :] = jnp.broadcast_to(
                        jnp.sum(sums[...] * ro_ref[...], axis=1, keepdims=True), (8, 128)
                    )
                yield

    pieces = unique()

    def work(n):
        for _ in range(n):
            next(pieces, None)

    work(4)
    wait(go_b, go_i)
    go_b = wire.start("x", lambda p: b1.at[:, :, p], b2.at[:, :, mx])
    go_i = wire.start("x", lambda p: ag.at[:, my, mk, mx], ag.at[:, my, mk, mx])
    b2[:, :, mx] = b1[:, :, mx]
    work(2)
    wait(go_a)
    go_a = wire.start("y", lambda p: a1.at[:, p], a2.at[:, my])
    a2[:, my] = a1[:, my]
    work(2)
    wait(go_b, go_i)
    go_b = wire.start("z", lambda p: b2.at[p], fb.at[mz, :, mk])
    fb[mz, :, mk] = b2[mz]
    work(2)
    wait(go_a)
    go_a = wire.start("x", lambda p: a2.at[:, :, p], fa.at[:, :, mk, mx])
    go_i = wire.start("y", lambda p: ag.at[:, my, mk], ag.at[:, my, mk])
    fa[:, :, mk, mx] = a2[:, :, mx]
    work(4)
    wait(go_a)
    go_a = wire.start("k", lambda p: fa.at[:, :, mk], fa.at[:, :, mk])
    wait(go_b, go_i)
    go_b = wire.start("k", lambda p: fb.at[:, :, mk], fb.at[:, :, mk])
    go_i = wire.start("k", lambda p: ag.at[:, :, mk], ag.at[:, :, mk])
    work(2)
    wait(go_a, go_b)

    center((fa, fb), xc, xn, xt)
    gram_rows(owner_ref, mk, xc, left)
    gram_part(left, xt, ga, gb)

    go_a = wire.start("x", lambda p: ga.at[:, :, p], ra1.at[mx])
    go_b = wire.start("y", lambda p: gb.at[:, p], rb1.at[my])
    wait(go_i)

    def widen(z, carry):
        agf[pl.ds(z * 256, 256), :] = ag[z].reshape(256, 128).astype(F32)
        return carry

    lax.fori_loop(0, NZ, widen, 0)
    for r in range(8):
        rows = pl.ds(32 * r, 32)
        v = [agf[pl.ds(256 * r + row, 32, stride=8), :] for row in range(7)]
        dense[0, rows, :] = v[0]
        dense[1, rows, :] = v[1]
        dense[2, rows, :] = v[2]
        dense[3, rows, :] = v[3] + v[4] + v[5]
        dense[4, rows, :] = v[6]
    work(20)

    mine = (((mz * NY + my) * NK + mk) * NX + mx).astype(F32)
    place = iota((32, 128), 0) == lax.div(iota((32, 128), 1), 4)
    hop, site = [], []
    for r in range(8):
        rows = pl.ds(32 * r, 32)
        local = dense[1, rows, :]
        pick = jnp.zeros((32, 128), F32)
        for u in range(32):
            pick = jnp.where(local == u, uv[u : u + 1, :], pick)
        known = dense[0, rows, :] == mine
        value = jnp.where(known, pick - dense[3, rows, :], 0.0)
        value = jnp.where(known, dense[2, rows, :] * jnp.exp(value), 0.0)
        for shift in (4, 8, 16, 32, 64):
            value = value + pltpu.roll(value, shift, 1)
        hop.append(jnp.sum(jnp.where(place, value, 0.0), axis=0, keepdims=True))
        site.append(jnp.sum(jnp.where(place, dense[4, rows, :], 0.0), axis=0, keepdims=True))
    part[0] = jnp.concatenate(hop, axis=0)
    go_e = wire.start("z", lambda p: part.at[0], arz.at[mz])

    wait(go_a, go_b)
    add_outer(lambda z: ga[z, :, mx], ra1, ga2, mx, NX)
    add_outer(lambda z: gb[z, my], rb1, gb2, my, NY)
    go_a = wire.start("y", lambda p: ga2.at[:, p], ra2.at[my])
    go_b = wire.start("x", lambda p: gb2.at[:, p], rb2.at[mx])
    wait(go_e)
    part[1] = add_inner(part[0], arz, mz, NZ)
    go_e = wire.start("y", lambda p: part.at[1], ary.at[my])
    wait(go_a, go_b)
    ga3[...] = add_inner(ga2[:, my], ra2, my, NY).astype(BF16)
    gb3[...] = add_inner(gb2[:, mx], rb2, mx, NX).astype(BF16)
    go_a = wire.start("z", lambda p: ga3.at[p], ra3.at[mz])
    go_b = wire.start("z", lambda p: gb3.at[p], rb3.at[mz])
    wait(go_e)
    part[2] = add_inner(part[1], ary, my, NY)
    go_e = wire.start("x", lambda p: part.at[2], arx.at[mx])
    wait(go_e)
    part[3] = add_inner(part[2], arx, mx, NX)
    go_e = wire.start("k", lambda p: part.at[3], ark.at[mk])
    wait(go_e)
    hopping = add_inner(part[3], ark, mk, NK)
    energy = jnp.concatenate(site, axis=0) - hopping
    energy_ref[...] = energy
    shifted = energy - jnp.sum(energy) / N_S
    high = shifted.astype(BF16)
    rest = shifted - high.astype(F32)
    middle = rest.astype(BF16)
    low = (rest - middle.astype(F32)).astype(BF16)
    three = jnp.concatenate([high, middle, low], axis=0)
    force = jnp.zeros((8, 256), F32)
    for r in range(8):
        out = jnp.dot(three, xn[mk, pl.ds(128 * r, 128), :], preferred_element_type=F32)
        out = out[0:8] + out[8:16] + out[16:24]
        force = force + jnp.where(iota((8, 256), 0) == r, out, 0.0)
    force_ref[...] = jnp.sum(force, axis=0, keepdims=True) / N_S

    wait(go_a, go_b)
    one = add_inner(ga3[mz], ra3, mz, NZ)
    two = add_inner(gb3[mz], rb3, mz, NZ)
    for h in range(2):
        gram_ref[:, 512 * h : 512 * h + 256] = one[4 * h : 4 * h + 4]
        gram_ref[:, 512 * h + 256 : 512 * h + 512] = two[4 * h : 4 * h + 4]


def body(sample_occ, unique_occ, conn_index, hop_sign, gram_owner, embed, kernels, weights, biases, readout):
    vmem = pl.BlockSpec(memory_space=pltpu.VMEM)
    smem = pl.BlockSpec(memory_space=pltpu.SMEM)
    grid = (NZ, NY, NX, 8, 128)
    energy, gram, force = pl.pallas_call(
        kernel,
        out_shape=(
            jax.ShapeDtypeStruct((8, 128), F32),
            jax.ShapeDtypeStruct((4, N_S), F32),
            jax.ShapeDtypeStruct((1, 256), F32),
        ),
        in_specs=[smem] + [vmem] * 9,
        out_specs=(vmem, vmem, vmem),
        scratch_shapes=[
            pltpu.VMEM((8, 256, 128), BF16),
            pltpu.VMEM((160, 512), BF16),
            pltpu.VMEM((12, 16, 128), F32),
            pltpu.VMEM((20, 16, 128), F32),
            pltpu.VMEM((12, 16, 8, 256), F32),
            pltpu.VMEM((20, 16, 8, 256), F32),
            pltpu.VMEM((25, 8, 256), F32),
            pltpu.VMEM((2, 128, 256), BF16),
            pltpu.VMEM((8, 256), F32),
            pltpu.VMEM((2, 1024, 128), F32),
            pltpu.VMEM((2, 1024, 128), F32),
            pltpu.VMEM((2, 2048, 128), F32),
            pltpu.VMEM((2, 256, 8, 128), F32),
            pltpu.VMEM((2, 1024, 256), BF16),
            pltpu.VMEM((2, NZ, 256, 128), BF16),
            pltpu.VMEM((2, 128, 8, 256), F32),
            pltpu.VMEM((32, 128), F32),
            pltpu.VMEM((5, 256, 128), F32),
            pltpu.VMEM((4, 8, 128), F32),
        ]
        + [pltpu.VMEM(grid, BF16)] * 6
        + [pltpu.VMEM((NZ, NY, NK, NX, 8, 128), BF16)] * 3
        + [pltpu.VMEM((2048, 128), F32)]
        + [pltpu.VMEM((NZ, NY, NX, 8, 256), BF16)] * 2
        + [pltpu.VMEM((4, NZ, 4, 8, 256), BF16)] * 2
        + [pltpu.VMEM((NZ, 4, 8, 256), BF16)] * 2
        + [pltpu.VMEM((4, NZ, 8, 256), BF16)] * 2
        + [pltpu.VMEM((NZ, 8, 256), BF16)] * 4
        + [pltpu.VMEM((n, 8, 128), F32) for n in (NZ, NY, NX, NK)]
        + [pltpu.SemaphoreType.DMA((96,)), pltpu.SemaphoreType.DMA((96,))],
        compiler_params=pltpu.CompilerParams(
            collective_id=0, has_side_effects=True, vmem_limit_bytes=48 << 20
        ),
        name="local_energy_gram",
    )(
        gram_owner, sample_occ, unique_occ, conn_index, hop_sign, embed, kernels, weights, biases,
        readout.reshape(1, 256),
    )
    mine = lax.axis_index(("eval", "blk"))
    return lax.dynamic_slice_in_dim(energy.reshape(N_S), 4 * mine, 4), gram, force.reshape(256)


def solution(mesh):
    both = ("eval", "blk")
    return jax.shard_map(
        body,
        mesh=mesh,
        in_specs=(P(both), P(both), P(both), P(both), P(), P(), P(), P(), P(), P()),
        out_specs=(P(both), P(both), P(both)),
        check_vma=False,
    )
```

```python
import jax
import jax.numpy as jnp
from jax import lax
from jax.experimental import pallas as pl
from jax.experimental.pallas import tpu as pltpu
from jax.sharding import PartitionSpec as P

MESH = pl.DeviceIdType.MESH
PLANES = (("z", "k"), ("y", "x"))
F32 = jnp.float32
BF16 = jnp.bfloat16
NZ, NY, NX, NK = 8, 4, 4, 2
N_S = 1024
WORK = (8, 3, 3, 3, 6, 3)
T0 = (((0,), (0,)), ((), ()))
NT = (((1,), (1,)), ((), ()))


def iota(shape, dim):
    return lax.broadcasted_iota(jnp.int32, shape, dim)


def spread_table(spread_ref):
    site, lane = iota((256, 128), 0), iota((256, 128), 1)
    same = lax.rem(site, 16) == lax.div(lane, 8)
    for c in range(8):
        hit = jnp.logical_and(same, lax.rem(lane, 8) == c)
        spread_ref[c] = jnp.where(hit, 1.0, 0.0).astype(BF16)


def occupied(occ_ref, first, spread_ref, rows, split):
    total = None
    sub, lane = iota((1, 8, 256), 1), iota((rows, 8, 256), 2)
    for c in range(8):
        o = occ_ref[first + (c % 4 if split else c)].astype(F32)
        o = jnp.where(lax.rem(sub, 2) == 0, o[0:1, :][None], o[1:2, :][None])
        row = lax.rem(iota((rows, 8, 256), 0) + (14 + (8 * (c // 4) if split else 0)), 16)
        o = jnp.where(lax.div(lane, 16) == row, o, 0.0).reshape(rows * 8, 256).astype(BF16)
        part = jnp.dot(o, spread_ref[c], preferred_element_type=F32)
        total = part if total is None else total + part
    return total.reshape(rows, 8, 128)


def patch_rows(t, zed_ref, rows):
    sub = iota((rows, 8, 128), 1)
    r = [t if dy == 2 else pltpu.roll(t, (8 * (2 - dy)) % 128, 2) for dy in range(5)]
    first = jnp.where(sub < 2, r[0], jnp.where(sub < 4, r[1], jnp.where(sub < 6, r[2], r[3])))
    second = jnp.where(sub < 2, r[4], jnp.where(sub == 2, 1.0, 0.0))
    zed_ref[:, 0:8, :] = first
    zed_ref[:, 8:16, :] = second


def tap_weights(embed_ref, k_ref, wz_ref):
    sub = iota((8, 256), 0)
    spin = jnp.where(lax.rem(sub, 2) == 0, embed_ref[0:1, :], embed_ref[1:2, :])
    const = embed_ref[2:3, :] * jnp.sum(k_ref[...], axis=0)[0:1, :]
    for dx in range(5):
        k = [k_ref[dx * 5 + dy, 0:1, :] for dy in range(5)]
        top = jnp.where(sub < 2, k[0], jnp.where(sub < 4, k[1], jnp.where(sub < 6, k[2], k[3]))) * spin
        low = jnp.where(sub < 2, k[4] * spin, jnp.where(sub == 2, const, 0.0) if dx == 0 else 0.0)
        own = jnp.where(lax.div(sub, 2) == 2, spin, 0.0) if dx == 2 else jnp.zeros((8, 256), F32)
        one = jnp.where(sub == 2, embed_ref[2:3, :], 0.0) if dx == 0 else jnp.zeros((8, 256), F32)
        base = jnp.concatenate(
            [jnp.concatenate([top, low], axis=0), jnp.concatenate([own, one], axis=0)], axis=1
        )
        high = base.astype(BF16)
        wz_ref[16 * dx : 16 * dx + 16, :] = high
        wz_ref[80 + 16 * dx : 96 + 16 * dx, :] = (base - high.astype(F32)).astype(BF16)


def first_layer(zed_ref, wz_ref, w_ref, b_ref, state_ref, low, high):
    many = 4

    def step(i, carry):
        xs = [i * many + k for k in range(many)]
        cols = []
        for x in xs:
            taps = [zed_ref[x + j].astype(BF16) for j in range(5)]
            cols.append(jnp.concatenate(taps + taps, axis=0))
        cols = jnp.concatenate(cols, axis=1)
        both = lax.dot_general(cols, wz_ref[...], T0, preferred_element_type=F32)
        mixed = both[:, :256].astype(BF16)
        pre = jnp.dot(mixed, w_ref[0], preferred_element_type=F32) + b_ref[0:1, :]
        half = 0.5 * pre
        new = both[:, 256:] + (half + half * jnp.tanh(half))
        state_ref[pl.ds(i * many + 2, many)] = new.reshape(many, 16, 8, 256)
        return carry

    lax.fori_loop(low // many, high // many, step, 0)


def halo(state_ref, rows, swap):
    for i in (0, 1):
        low = state_ref[rows + i]
        high = state_ref[2 + i]
        if swap:
            low = pltpu.roll(low, 4, 1)
            high = pltpu.roll(high, 4, 1)
        state_ref[i] = low
        state_ref[rows + 2 + i] = high


def convolve(state_ref, kb_ref, x):
    halves = []
    for h in range(2):
        lanes = slice(128 * h, 128 * h + 128)
        acc = None
        for dx in range(5):
            row = state_ref[x + dx, :, :, lanes]
            for dy in range(5):
                s = (dy - 2) % 16
                moved = row if s == 0 else jnp.concatenate([row[s:], row[:s]], axis=0)
                term = moved * kb_ref[dx * 5 + dy, :, lanes][None]
                acc = term if acc is None else acc + term
        halves.append(acc.reshape(128, 128))
    return jnp.concatenate(halves, axis=1)


class SecondLayer:
    def __init__(self, state_ref, kb_ref, mix_ref, w_ref, b_ref, total_ref, rows, keep_mixed=None, keep_rest=None):
        self.state, self.kb, self.mix, self.w, self.b = state_ref, kb_ref, mix_ref, w_ref, b_ref
        self.total, self.rows, self.keep_mixed, self.keep_rest = total_ref, rows, keep_mixed, keep_rest

    def finish(self, x, total):
        pre = jnp.dot(self.mix[lax.rem(x, 2)], self.w[1], preferred_element_type=F32) + self.b[1:2, :]
        half = 0.5 * pre
        th_half = jnp.tanh(half)
        out = jnp.tanh(self.state[x + 2].reshape(128, 256) + (half + half * th_half))
        if self.keep_rest is not None:
            self.keep_rest(x, pre, th_half, out)
        return total + jnp.sum(out.reshape(16, 8, 256), axis=0)

    def make(self, x):
        mixed = convolve(self.state, self.kb, x)
        self.mix[lax.rem(x, 2)] = mixed.astype(BF16)
        if self.keep_mixed is not None:
            self.keep_mixed(x, mixed)

    def part(self, low, high):
        if low == 0:
            self.make(jnp.int32(0))
            self.total[...] = jnp.zeros((8, 256), F32)

        def step(x, total):
            total = self.finish(x - 1, total)
            self.make(x)
            return total

        total = lax.fori_loop(max(low, 1), high, step, self.total[...])
        self.total[...] = self.finish(jnp.int32(high - 1), total) if high == self.rows else total


class Wire:
    def __init__(self, send, recv):
        e, x = lax.axis_index("eval"), lax.axis_index("blk")
        self.at = {
            "z": lax.div(e, NY * NK),
            "y": lax.rem(lax.div(e, NK), NY),
            "k": lax.rem(e, NK),
            "x": x,
        }
        self.size = {"z": NZ, "y": NY, "k": NK, "x": NX}
        self.send, self.recv, self.used = send, recv, 0

    def peer(self, axis, off):
        return lax.rem(self.at[axis] + off, self.size[axis])

    def device(self, axis, place):
        at = {**self.at, axis: place}
        return ((at["z"] * NY + at["y"]) * NK + at["k"], at["x"])

    def member(self, axes, place):
        inner = self.size[axes[1]]
        at = {**self.at, axes[0]: lax.div(place, inner), axes[1]: lax.rem(place, inner)}
        return ((at["z"] * NY + at["y"]) * NK + at["k"], at["x"])

    def rank(self, axes):
        return self.at[axes[0]] * self.size[axes[1]] + self.at[axes[1]]

    def greet(self):
        sem = pltpu.get_barrier_semaphore()
        count = 0
        for axes in PLANES:
            many = self.size[axes[0]] * self.size[axes[1]]
            for off in range(1, many):
                place = lax.rem(self.rank(axes) + off, many)
                pl.semaphore_signal(sem, inc=1, device_id=self.member(axes, place), device_id_type=MESH)
                count += 1
        return sem, count

    def pair(self):
        self.used += 1
        return {"send_sem": self.send.at[self.used - 1], "recv_sem": self.recv.at[self.used - 1]}

    def end(self, sems, region, device):
        return pltpu.make_async_remote_copy(
            src_ref=region, dst_ref=region, device_id=device, device_id_type=MESH, **sems
        )

    def share(self, axes, src, dst_ref):
        many = self.size[axes[0]] * self.size[axes[1]]
        sems = self.pair()
        for off in range(1, many):
            device = self.member(axes, lax.rem(self.rank(axes) + off, many))
            pltpu.make_async_remote_copy(
                src_ref=src, dst_ref=dst_ref.at[self.rank(axes)], device_id=device, device_id_type=MESH, **sems
            ).start()
        return self.end(sems, dst_ref.at[0 : many - 1], device)

    def push(self, axis, src, dst, sems):
        for off in range(1, self.size[axis]):
            place = self.peer(axis, off)
            pltpu.make_async_remote_copy(
                src_ref=src(place),
                dst_ref=dst(self.at[axis]),
                device_id=self.device(axis, place),
                device_id_type=MESH,
                **sems,
            ).start()

    def start(self, axis, src, dst):
        sems = self.pair()
        self.push(axis, src, dst, sems)
        return self.end(sems, dst(pl.ds(0, self.size[axis] - 1)), self.device(axis, self.peer(axis, 1)))


def wait(*groups):
    for group in groups:
        group.wait()


def jacobian(mixf_ref, cotf_ref, jf_ref, send_refs):
    for s in range(4):
        rows = pl.ds(s, 256, stride=4)
        left = jnp.concatenate([mixf_ref[h, rows, :] for h in range(2)], axis=1).astype(BF16)
        right = jnp.concatenate([cotf_ref[h, rows, :] for h in range(2)], axis=1).astype(BF16)
        out = lax.dot_general(left, right, T0, preferred_element_type=F32)
        for h in range(2):
            jf_ref[h, pl.ds(s, 256, stride=8), :] = out[:, 128 * h : 128 * h + 128]
    low = iota((NY, NX, 8, 128), 2) < 4

    def step(z, carry):
        for h in range(2):
            t = jf_ref[h, pl.ds(z * 256, 256), :].reshape(NY, NK, NX, 8, 128)
            send_refs[h][z] = jnp.where(low, t[:, 0], pltpu.roll(t[:, 1], 4, 2)).astype(BF16)
        return carry

    lax.fori_loop(0, NZ, step, 0)


def center(full_refs, xc_ref, xn_ref, xt_ref):
    for h in range(2):

        def add(z, total):
            return total + jnp.sum(full_refs[h][z].reshape(32, 8, 128).astype(F32), axis=0)

        total = lax.fori_loop(0, NZ, add, jnp.zeros((8, 128), F32))
        means = [jnp.sum(total[4 * k : 4 * k + 4], axis=0, keepdims=True) / N_S for k in range(2)]
        mean = jnp.where(iota((8, 128), 0) < 4, means[0], means[1])

        def step(z, carry):
            t = full_refs[h][z].reshape(32, 8, 128).astype(F32) - mean[None]
            t = t.astype(BF16).astype(F32)
            xc_ref[h, pl.ds(z * 32, 32)] = t
            t = t.reshape(16, 2, 8, 128)
            low = iota((16, 8, 128), 1) < 4
            one = jnp.where(low, t[:, 0], pltpu.roll(t[:, 1], 4, 1))
            two = jnp.where(low, pltpu.roll(t[:, 0], 4, 1), t[:, 1])
            for k, v in enumerate((one, two)):
                v = v.reshape(128, 128)
                xn_ref[k, pl.ds(z * 128, 128), 128 * h : 128 * h + 128] = v.astype(BF16)
                xt_ref[k, z, 128 * h : 128 * h + 128, :] = v.T.astype(BF16)
            return carry

        lax.fori_loop(0, NZ, step, 0)


def gram_rows(owner_ref, core, xc_ref, left_ref):
    low = iota((8, 128), 0) < 4

    def step(i, carry):
        for j in range(16):
            q = i * 16 + j
            own = owner_ref[i * (2 * NK * NX * 2) + (j // NX) * (NK * NX) + core * NX + j % NX]
            for h in range(2):
                t = xc_ref[h, own]
                r = pltpu.roll(t, 4, 0)
                left_ref[0, q, :, 128 * h : 128 * h + 128] = jnp.where(low, t, r)
                left_ref[1, q, :, 128 * h : 128 * h + 128] = jnp.where(low, r, t)
        return carry

    lax.fori_loop(0, NZ, step, 0)


def gram_part(left_ref, xt_ref, ga_ref, gb_ref, done):
    low = lax.rem(lax.div(iota((256, 256), 0), 4), 2) == 0

    def step(i, carry):
        rows = [left_ref[k, pl.ds(i * 32, 32)].reshape(256, 256).astype(BF16) for k in range(2)]

        def columns(c):
            out = None
            for k in range(2):
                right = jnp.concatenate([xt_ref[k, 2 * c], xt_ref[k, 2 * c + 1]], axis=1)
                part = jnp.dot(rows[k], right, preferred_element_type=F32)
                out = part if out is None else out + part
            return out

        for c, ref in enumerate((ga_ref, gb_ref)):
            out = jnp.where(low, columns(c), columns(c + 2)) * (1.0 / N_S)
            ref[pl.ds(2 * i, 2)] = out.astype(BF16).reshape(2, NY, NX, 8, 256)
        done(pl.ds(2 * i, 2))
        return carry

    lax.fori_loop(0, NZ // 2, step, 0)


def add_outer(own, got_ref, out_ref, at, size):
    def step(z, carry):
        total = own(z).astype(F32)
        for off in range(1, size):
            total = total + got_ref[lax.rem(at + off, size), z].astype(F32)
        out_ref[z] = total.astype(BF16)
        return carry

    lax.fori_loop(0, NZ, step, 0)


def add_inner(own, got_ref, at, size):
    total = own.astype(F32)
    for off in range(1, size):
        total = total + got_ref[lax.rem(at + off, size)].astype(F32)
    return total


def own_info(index_ref, sign_ref, occ_ref, amp):
    sub, lane = iota((4, 128), 0), iota((4, 128), 1)
    pick = jnp.where(iota((32, 128), 0) == lax.div(iota((32, 128), 1), 4), 1.0, 0.0).astype(BF16)
    mine = sub == lax.rem(lane, 4)

    def row(v):
        v = jnp.dot(v.astype(F32).astype(BF16), pick, preferred_element_type=F32)
        return jnp.sum(jnp.where(mine, v, 0.0), axis=0, keepdims=True)

    index = index_ref[...]
    rows = [row(lax.shift_right_logical(index, 5)), row(jnp.bitwise_and(index, 31)), row(2 * sign_ref[...] - 1)]
    whole = jnp.sum(jnp.where(iota((8, 128), 0) == lax.rem(iota((8, 128), 1), 4), amp, 0.0), axis=0, keepdims=True)
    for _ in range(3):
        part = whole.astype(BF16).astype(F32)
        rows.append(part)
        whole = whole - part
    site = jnp.zeros((1, 128), F32)
    for i in range(4):
        o = occ_ref[i].astype(F32) - 0.5
        value = 4.0 * jnp.sum(o[0:1, :] * o[1:2, :], axis=1, keepdims=True)
        site = jnp.where(lax.rem(iota((1, 128), 1), 4) == i, value, site)
    rows += [site, jnp.zeros((1, 128), F32)]
    return jnp.concatenate(rows, axis=0).astype(BF16)


def kernel(
    owner_hbm, occ_s_hbm, occ_u_hbm, index_hbm, sign_hbm, embed_hbm, k_hbm, w_hbm, b_hbm, ro_hbm,
    energy_hbm, gram_hbm, force_hbm,
    owner_ref, energy_ref, gram_ref, force_ref, occ_s_ref, occ_u_ref, index_ref, sign_ref, embed_ref, k_ref, w_ref, b_ref, ro_ref,
    spread, wz, zs, zu, ss, su, kb, mix, sums, mixf, cotf, jf, xc, xn, xt, left, uv, dense, part,
    a0, a1, a2, b0, b1, b2, fa, fb, ag, agf,
    ga, gb, ra1, rb1, ga2, gb2, ra2, rb2, ga3, gb3, ra3, rb3,
    ar_one, ar_two,
    send, recv, near,
):
    wire = Wire(send, recv)
    mz, my, mk, mx = (wire.at[a] for a in "zykx")
    fetched = [
        pltpu.make_async_copy(src, dst, near.at[i])
        for i, (src, dst) in enumerate(
            (
                (k_hbm, k_ref), (embed_hbm, embed_ref), (occ_s_hbm, occ_s_ref), (b_hbm, b_ref), (ro_hbm, ro_ref),
                (w_hbm, w_ref), (occ_u_hbm, occ_u_ref), (index_hbm, index_ref), (sign_hbm, sign_ref), (owner_hbm, owner_ref),
            )
        )
    ]
    for copy in fetched:
        copy.start()
    entry, count = wire.greet()
    spread_table(spread)
    for copy in fetched[:6]:
        copy.wait()
    for t in range(25):
        kb[t] = jnp.broadcast_to(k_ref[t, 1:2, :], (8, 256))
    tap_weights(embed_ref, k_ref, wz)

    patch_rows(occupied(occ_s_ref, 0, spread, 12, True), zs, 12)
    first_layer(zs, wz, w_ref, b_ref, ss, 0, 8)
    halo(ss, 8, True)

    def keep_mixed(x, mixed):
        for h in range(2):
            mixf[h, pl.ds(x * 128, 128), :] = mixed[:, 128 * h : 128 * h + 128].astype(BF16).astype(F32)

    def keep_cot(x, pre, th, out):
        g = 0.5 + 0.5 * th
        cot = ro_ref[...] * (1.0 - out * out) * (g * (1.0 + pre * (1.0 - g)))
        for h in range(2):
            cotf[h, pl.ds(x * 128, 128), :] = cot[:, 128 * h : 128 * h + 128].astype(BF16).astype(F32)

    SecondLayer(ss, kb, mix, w_ref, b_ref, sums, 8, keep_mixed, keep_cot).part(0, 8)
    jacobian(mixf, cotf, jf, (a0, b0))
    for copy in fetched[6:]:
        copy.wait()
    pl.semaphore_wait(entry, count)

    go_a = wire.start("z", lambda p: a0.at[p], lambda p: a1.at[p])
    go_b = wire.start("y", lambda p: b0.at[:, p], lambda p: b1.at[:, p])
    amp = jnp.broadcast_to(jnp.sum(sums[...] * ro_ref[...], axis=1, keepdims=True), (8, 128))
    amp = amp + pltpu.roll(amp, 4, 0)
    ag[mz, my, mk, mx] = own_info(index_ref, sign_ref, occ_s_ref, amp)
    go_i = wire.start("z", lambda p: ag.at[mz, my, mk, mx], lambda p: ag.at[p, my, mk, mx])
    a1[mz] = a0[mz]
    b1[:, my] = b0[:, my]

    layer = SecondLayer(su, kb, mix, w_ref, b_ref, sums, 16)

    def unique():
        for g in range(4):
            patch_rows(occupied(occ_u_ref, 8 * g, spread, 20, False), zu, 20)
            yield
            first_layer(zu, wz, w_ref, b_ref, su, 0, 8)
            yield
            first_layer(zu, wz, w_ref, b_ref, su, 8, 16)
            halo(su, 16, False)
            yield
            for x in range(0, 16, 4):
                layer.part(x, x + 4)
                if x == 12:
                    uv[8 * g : 8 * g + 8, :] = jnp.broadcast_to(
                        jnp.sum(sums[...] * ro_ref[...], axis=1, keepdims=True), (8, 128)
                    )
                yield

    pieces = unique()

    def work(n):
        for _ in range(n):
            next(pieces, None)

    work(WORK[0])
    wait(go_b, go_i)
    go_b = wire.start("x", lambda p: b1.at[:, :, p], lambda p: b2.at[:, :, p])
    go_i = wire.start("x", lambda p: ag.at[:, my, mk, mx], lambda p: ag.at[:, my, mk, p])
    b2[:, :, mx] = b1[:, :, mx]
    work(WORK[1])
    wait(go_a)
    go_a = wire.start("y", lambda p: a1.at[:, p], lambda p: a2.at[:, p])
    a2[:, my] = a1[:, my]
    work(WORK[2])
    wait(go_b, go_i)
    go_b = wire.start("z", lambda p: b2.at[p], lambda p: fb.at[p, :, mk])
    fb[mz, :, mk] = b2[mz]
    work(WORK[3])
    wait(go_a)
    go_a = wire.start("x", lambda p: a2.at[:, :, p], lambda p: fa.at[:, :, mk, p])
    go_i = wire.start("y", lambda p: ag.at[:, my, mk], lambda p: ag.at[:, p, mk])
    fa[:, :, mk, mx] = a2[:, :, mx]
    work(WORK[4])
    wait(go_a)
    go_a = wire.start("k", lambda p: fa.at[:, :, mk], lambda p: fa.at[:, :, p])
    wait(go_b)
    go_b = wire.start("k", lambda p: fb.at[:, :, mk], lambda p: fb.at[:, :, p])
    work(WORK[5])
    wait(go_i, go_a, go_b)
    go_i = wire.start("k", lambda p: ag.at[:, :, mk], lambda p: ag.at[:, :, p])

    center((fa, fb), xc, xn, xt)
    gram_rows(owner_ref, mk, xc, left)
    sems_a, sems_b = wire.pair(), wire.pair()

    def done(z):
        wire.push("x", lambda p: ga.at[z, :, p], lambda p: ra1.at[p, z], sems_a)
        wire.push("y", lambda p: gb.at[z, p], lambda p: rb1.at[p, z], sems_b)

    gram_part(left, xt, ga, gb, done)
    go_a = wire.end(sems_a, ra1.at[0:3], wire.device("x", wire.peer("x", 1)))
    go_b = wire.end(sems_b, rb1.at[0:3], wire.device("y", wire.peer("y", 1)))
    wait(go_i)

    def widen(z, carry):
        agf[pl.ds(z * 256, 256), :] = ag[z].reshape(256, 128).astype(F32)
        return carry

    lax.fori_loop(0, NZ, widen, 0)
    for r in range(8):
        rows = pl.ds(32 * r, 32)
        v = [agf[pl.ds(256 * r + row, 32, stride=8), :] for row in range(7)]
        dense[0, rows, :] = v[0]
        dense[1, rows, :] = v[1]
        dense[2, rows, :] = v[2]
        dense[3, rows, :] = v[3] + v[4] + v[5]
        dense[4, rows, :] = v[6]
    work(28)

    mine = (((mz * NY + my) * NK + mk) * NX + mx).astype(F32)
    place = iota((32, 128), 0) == lax.div(iota((32, 128), 1), 4)
    hop, site = [], []
    for r in range(8):
        rows = pl.ds(32 * r, 32)
        local = dense[1, rows, :]
        pick = jnp.zeros((32, 128), F32)
        for u in range(32):
            pick = jnp.where(local == u, uv[u : u + 1, :], pick)
        known = dense[0, rows, :] == mine
        value = jnp.where(known, pick - dense[3, rows, :], 0.0)
        value = jnp.where(known, dense[2, rows, :] * jnp.exp(value), 0.0)
        for shift in (4, 8, 16, 32, 64):
            value = value + pltpu.roll(value, shift, 1)
        hop.append(jnp.sum(jnp.where(place, value, 0.0), axis=0, keepdims=True))
        site.append(jnp.sum(jnp.where(place, dense[4, rows, :], 0.0), axis=0, keepdims=True))
    part[0] = jnp.concatenate(hop, axis=0)
    go_e = wire.share(PLANES[0], part.at[0], ar_one)

    wait(go_a, go_b)
    add_outer(lambda z: ga[z, :, mx], ra1, ga2, mx, NX)
    add_outer(lambda z: gb[z, my], rb1, gb2, my, NY)
    go_a = wire.start("y", lambda p: ga2.at[:, p], lambda p: ra2.at[p])
    go_b = wire.start("x", lambda p: gb2.at[:, p], lambda p: rb2.at[p])
    wait(go_e)
    part[1] = add_inner(part[0], ar_one, wire.rank(PLANES[0]), NZ * NK)
    go_e = wire.share(PLANES[1], part.at[1], ar_two)
    wait(go_a, go_b)
    ga3[...] = add_inner(ga2[:, my], ra2, my, NY).astype(BF16)
    gb3[...] = add_inner(gb2[:, mx], rb2, mx, NX).astype(BF16)
    go_a = wire.start("z", lambda p: ga3.at[p], lambda p: ra3.at[p])
    go_b = wire.start("z", lambda p: gb3.at[p], lambda p: rb3.at[p])
    wait(go_e)
    hopping = add_inner(part[1], ar_two, wire.rank(PLANES[1]), NY * NX)
    energy = jnp.concatenate(site, axis=0) - hopping
    energy_ref[...] = energy
    leave = [pltpu.make_async_copy(energy_ref, energy_hbm, near.at[0])]
    leave[0].start()
    shifted = energy - jnp.sum(energy) / N_S
    high = shifted.astype(BF16)
    rest = shifted - high.astype(F32)
    middle = rest.astype(BF16)
    low = (rest - middle.astype(F32)).astype(BF16)
    three = jnp.concatenate([high, middle, low], axis=0)
    force = jnp.zeros((8, 256), F32)
    for r in range(8):
        out = jnp.dot(three, xn[mk, pl.ds(128 * r, 128), :], preferred_element_type=F32)
        out = out[0:8] + out[8:16] + out[16:24]
        force = force + jnp.where(iota((8, 256), 0) == r, out, 0.0)
    force_ref[...] = jnp.sum(force, axis=0, keepdims=True) / N_S
    leave.append(pltpu.make_async_copy(force_ref, force_hbm, near.at[1]))
    leave[1].start()

    wait(go_a, go_b)
    one = add_inner(ga3[mz], ra3, mz, NZ)
    two = add_inner(gb3[mz], rb3, mz, NZ)
    for h in range(2):
        gram_ref[:, 512 * h : 512 * h + 256] = one[4 * h : 4 * h + 4]
        gram_ref[:, 512 * h + 256 : 512 * h + 512] = two[4 * h : 4 * h + 4]
    leave.append(pltpu.make_async_copy(gram_ref, gram_hbm, near.at[2]))
    leave[2].start()
    wait(*leave)


def body(sample_occ, unique_occ, conn_index, hop_sign, gram_owner, embed, kernels, weights, biases, readout):
    grid = (NZ, NY, NX, 8, 128)
    operands = (
        sample_occ, unique_occ, conn_index, hop_sign, embed, kernels.transpose(1, 0, 2),
        weights, biases, readout.reshape(1, 256),
    )
    energy, gram, force = pl.pallas_call(
        kernel,
        out_shape=(
            jax.ShapeDtypeStruct((8, 128), F32),
            jax.ShapeDtypeStruct((4, N_S), F32),
            jax.ShapeDtypeStruct((1, 256), F32),
        ),
        in_specs=[pl.BlockSpec(memory_space=pl.ANY)] * 10,
        out_specs=(pl.BlockSpec(memory_space=pl.ANY),) * 3,
        scratch_shapes=[
            pltpu.SMEM((256,), jnp.int32),
            pltpu.VMEM((8, 128), F32),
            pltpu.VMEM((4, N_S), F32),
            pltpu.VMEM((1, 256), F32),
        ]
        + [pltpu.VMEM(v.shape, v.dtype) for v in operands]
        + [
            pltpu.VMEM((8, 256, 128), BF16),
            pltpu.VMEM((160, 512), BF16),
            pltpu.VMEM((12, 16, 128), F32),
            pltpu.VMEM((20, 16, 128), F32),
            pltpu.VMEM((12, 16, 8, 256), F32),
            pltpu.VMEM((20, 16, 8, 256), F32),
            pltpu.VMEM((25, 8, 256), F32),
            pltpu.VMEM((2, 128, 256), BF16),
            pltpu.VMEM((8, 256), F32),
            pltpu.VMEM((2, 1024, 128), F32),
            pltpu.VMEM((2, 1024, 128), F32),
            pltpu.VMEM((2, 2048, 128), F32),
            pltpu.VMEM((2, 256, 8, 128), F32),
            pltpu.VMEM((2, 1024, 256), BF16),
            pltpu.VMEM((2, NZ, 256, 128), BF16),
            pltpu.VMEM((2, 128, 8, 256), F32),
            pltpu.VMEM((32, 128), F32),
            pltpu.VMEM((5, 256, 128), F32),
            pltpu.VMEM((2, 8, 128), F32),
        ]
        + [pltpu.VMEM(grid, BF16)] * 6
        + [pltpu.VMEM((NZ, NY, NK, NX, 8, 128), BF16)] * 3
        + [pltpu.VMEM((2048, 128), F32)]
        + [pltpu.VMEM((NZ, NY, NX, 8, 256), BF16)] * 2
        + [pltpu.VMEM((4, NZ, 4, 8, 256), BF16)] * 2
        + [pltpu.VMEM((NZ, 4, 8, 256), BF16)] * 2
        + [pltpu.VMEM((4, NZ, 8, 256), BF16)] * 2
        + [pltpu.VMEM((NZ, 8, 256), BF16)] * 4
        + [pltpu.VMEM((16, 8, 128), F32)] * 2
        + [pltpu.SemaphoreType.DMA((n,)) for n in (20, 20, 10)],
        compiler_params=pltpu.CompilerParams(
            collective_id=0, has_side_effects=True, vmem_limit_bytes=60 << 20
        ),
        name="local_energy_gram",
    )(gram_owner, *operands)
    mine = lax.axis_index(("eval", "blk"))
    return lax.dynamic_slice_in_dim(energy.reshape(N_S), 4 * mine, 4), gram, force.reshape(256)


def solution(mesh):
    both = ("eval", "blk")
    return jax.shard_map(
        body,
        mesh=mesh,
        in_specs=(P(both), P(both), P(both), P(both), P(), P(), P(), P(), P(), P()),
        out_specs=(P(both), P(both), P(both)),
        check_vma=False,
    )
```

```python
import jax
import jax.numpy as jnp
from jax import lax
from jax.experimental import pallas as pl
from jax.experimental.pallas import tpu as pltpu
from jax.sharding import PartitionSpec as P

MESH = pl.DeviceIdType.MESH
PLANES = (("z", "k"), ("y", "x"))
F32 = jnp.float32
BF16 = jnp.bfloat16
NZ, NY, NX, NK = 8, 4, 4, 2
N_S = 1024
WORK = (8, 3, 3, 3, 6, 1)
T0 = (((0,), (0,)), ((), ()))
NT = (((1,), (1,)), ((), ()))


def iota(shape, dim):
    return lax.broadcasted_iota(jnp.int32, shape, dim)


def spread_table(spread_ref):
    site, lane = iota((256, 128), 0), iota((256, 128), 1)
    same = lax.rem(site, 16) == lax.div(lane, 8)
    for c in range(8):
        hit = jnp.logical_and(same, lax.rem(lane, 8) == c)
        spread_ref[c] = jnp.where(hit, 1.0, 0.0).astype(BF16)


def occupied(occ_ref, first, spread_ref, rows, split):
    total = None
    sub, lane = iota((1, 8, 256), 1), iota((rows, 8, 256), 2)
    for c in range(8):
        o = occ_ref[first + (c % 4 if split else c)].astype(F32)
        o = jnp.where(lax.rem(sub, 2) == 0, o[0:1, :][None], o[1:2, :][None])
        row = lax.rem(iota((rows, 8, 256), 0) + (14 + (8 * (c // 4) if split else 0)), 16)
        o = jnp.where(lax.div(lane, 16) == row, o, 0.0).reshape(rows * 8, 256).astype(BF16)
        part = jnp.dot(o, spread_ref[c], preferred_element_type=F32)
        total = part if total is None else total + part
    return total.reshape(rows, 8, 128)


def patch_rows(t, zed_ref, rows):
    sub = iota((rows, 8, 128), 1)
    r = [t if dy == 2 else pltpu.roll(t, (8 * (2 - dy)) % 128, 2) for dy in range(5)]
    first = jnp.where(sub < 2, r[0], jnp.where(sub < 4, r[1], jnp.where(sub < 6, r[2], r[3])))
    second = jnp.where(sub < 2, r[4], jnp.where(sub == 2, 1.0, 0.0))
    zed_ref[:, 0:8, :] = first
    zed_ref[:, 8:16, :] = second


def tap_weights(embed_ref, k_ref, wz_ref):
    sub = iota((8, 256), 0)
    spin = jnp.where(lax.rem(sub, 2) == 0, embed_ref[0:1, :], embed_ref[1:2, :])
    const = embed_ref[2:3, :] * jnp.sum(k_ref[...], axis=0)[0:1, :]
    for dx in range(5):
        k = [k_ref[dx * 5 + dy, 0:1, :] for dy in range(5)]
        top = jnp.where(sub < 2, k[0], jnp.where(sub < 4, k[1], jnp.where(sub < 6, k[2], k[3]))) * spin
        low = jnp.where(sub < 2, k[4] * spin, jnp.where(sub == 2, const, 0.0) if dx == 0 else 0.0)
        own = jnp.where(lax.div(sub, 2) == 2, spin, 0.0) if dx == 2 else jnp.zeros((8, 256), F32)
        one = jnp.where(sub == 2, embed_ref[2:3, :], 0.0) if dx == 0 else jnp.zeros((8, 256), F32)
        base = jnp.concatenate(
            [jnp.concatenate([top, low], axis=0), jnp.concatenate([own, one], axis=0)], axis=1
        )
        high = base.astype(BF16)
        wz_ref[16 * dx : 16 * dx + 16, :] = high
        wz_ref[80 + 16 * dx : 96 + 16 * dx, :] = (base - high.astype(F32)).astype(BF16)


def first_layer(zed_ref, wz_ref, w_ref, b_ref, state_ref, low, high):
    many = 4

    def step(i, carry):
        xs = [i * many + k for k in range(many)]
        cols = []
        for x in xs:
            taps = [zed_ref[x + j].astype(BF16) for j in range(5)]
            cols.append(jnp.concatenate(taps + taps, axis=0))
        cols = jnp.concatenate(cols, axis=1)
        both = lax.dot_general(cols, wz_ref[...], T0, preferred_element_type=F32)
        mixed = both[:, :256].astype(BF16)
        pre = jnp.dot(mixed, w_ref[0], preferred_element_type=F32) + b_ref[0:1, :]
        half = 0.5 * pre
        new = both[:, 256:] + (half + half * jnp.tanh(half))
        state_ref[pl.ds(i * many + 2, many)] = new.reshape(many, 16, 8, 256)
        return carry

    lax.fori_loop(low // many, high // many, step, 0)


def halo(state_ref, rows, swap):
    for i in (0, 1):
        low = state_ref[rows + i]
        high = state_ref[2 + i]
        if swap:
            low = pltpu.roll(low, 4, 1)
            high = pltpu.roll(high, 4, 1)
        state_ref[i] = low
        state_ref[rows + 2 + i] = high


def convolve(state_ref, kb_ref, x):
    halves = []
    for h in range(2):
        lanes = slice(128 * h, 128 * h + 128)
        acc = None
        for dx in range(5):
            row = state_ref[x + dx, :, :, lanes]
            for dy in range(5):
                s = (dy - 2) % 16
                moved = row if s == 0 else jnp.concatenate([row[s:], row[:s]], axis=0)
                term = moved * kb_ref[dx * 5 + dy, :, lanes][None]
                acc = term if acc is None else acc + term
        halves.append(acc.reshape(128, 128))
    return jnp.concatenate(halves, axis=1)


class SecondLayer:
    def __init__(self, state_ref, kb_ref, mix_ref, w_ref, b_ref, total_ref, rows, keep_mixed=None, keep_rest=None):
        self.state, self.kb, self.mix, self.w, self.b = state_ref, kb_ref, mix_ref, w_ref, b_ref
        self.total, self.rows, self.keep_mixed, self.keep_rest = total_ref, rows, keep_mixed, keep_rest

    def finish(self, x, total):
        pre = jnp.dot(self.mix[lax.rem(x, 2)], self.w[1], preferred_element_type=F32) + self.b[1:2, :]
        half = 0.5 * pre
        th_half = jnp.tanh(half)
        out = jnp.tanh(self.state[x + 2].reshape(128, 256) + (half + half * th_half))
        if self.keep_rest is not None:
            self.keep_rest(x, pre, th_half, out)
        return total + jnp.sum(out.reshape(16, 8, 256), axis=0)

    def make(self, x):
        mixed = convolve(self.state, self.kb, x)
        self.mix[lax.rem(x, 2)] = mixed.astype(BF16)
        if self.keep_mixed is not None:
            self.keep_mixed(x, mixed)

    def part(self, low, high):
        if low == 0:
            self.make(jnp.int32(0))
            self.total[...] = jnp.zeros((8, 256), F32)

        def step(x, total):
            total = self.finish(x - 1, total)
            self.make(x)
            return total

        total = lax.fori_loop(max(low, 1), high, step, self.total[...])
        self.total[...] = self.finish(jnp.int32(high - 1), total) if high == self.rows else total


class Wire:
    def __init__(self, send, recv):
        e, x = lax.axis_index("eval"), lax.axis_index("blk")
        self.at = {
            "z": lax.div(e, NY * NK),
            "y": lax.rem(lax.div(e, NK), NY),
            "k": lax.rem(e, NK),
            "x": x,
        }
        self.size = {"z": NZ, "y": NY, "k": NK, "x": NX}
        self.send, self.recv, self.used = send, recv, 0

    def linear(self):
        return ((self.at["z"] * NY + self.at["y"]) * NK + self.at["k"]) * NX + self.at["x"]

    def peer(self, axis, off):
        return lax.rem(self.at[axis] + off, self.size[axis])

    def device(self, axis, place):
        at = {**self.at, axis: place}
        return ((at["z"] * NY + at["y"]) * NK + at["k"], at["x"])

    def member(self, axes, place):
        inner = self.size[axes[1]]
        at = {**self.at, axes[0]: lax.div(place, inner), axes[1]: lax.rem(place, inner)}
        return ((at["z"] * NY + at["y"]) * NK + at["k"], at["x"])

    def rank(self, axes):
        return self.at[axes[0]] * self.size[axes[1]] + self.at[axes[1]]

    def greet(self):
        sem = pltpu.get_barrier_semaphore()
        count = 0
        for axes in PLANES:
            many = self.size[axes[0]] * self.size[axes[1]]
            for off in range(1, many):
                place = lax.rem(self.rank(axes) + off, many)
                pl.semaphore_signal(sem, inc=1, device_id=self.member(axes, place), device_id_type=MESH)
                count += 1
        return sem, count

    def pair(self):
        self.used += 1
        return {"send_sem": self.send.at[self.used - 1], "recv_sem": self.recv.at[self.used - 1]}

    def end(self, sems, region, device):
        return pltpu.make_async_remote_copy(
            src_ref=region, dst_ref=region, device_id=device, device_id_type=MESH, **sems
        )

    def share(self, axes, src, dst_ref):
        many = self.size[axes[0]] * self.size[axes[1]]
        sems = self.pair()
        for off in range(1, many):
            device = self.member(axes, lax.rem(self.rank(axes) + off, many))
            pltpu.make_async_remote_copy(
                src_ref=src, dst_ref=dst_ref.at[self.rank(axes)], device_id=device, device_id_type=MESH, **sems
            ).start()
        return self.end(sems, dst_ref.at[0 : many - 1], device)

    def push(self, axis, src, dst, sems):
        for off in range(1, self.size[axis]):
            place = self.peer(axis, off)
            pltpu.make_async_remote_copy(
                src_ref=src(place),
                dst_ref=dst(self.at[axis]),
                device_id=self.device(axis, place),
                device_id_type=MESH,
                **sems,
            ).start()

    def start(self, axis, src, dst):
        sems = self.pair()
        self.push(axis, src, dst, sems)
        return self.end(sems, dst(pl.ds(0, self.size[axis] - 1)), self.device(axis, self.peer(axis, 1)))


def wait(*groups):
    for group in groups:
        group.wait()


def jacobian(mixf_ref, cotf_ref, jf_ref, send_refs):
    for s in range(4):
        rows = pl.ds(s, 256, stride=4)
        left = jnp.concatenate([mixf_ref[h, rows, :] for h in range(2)], axis=1).astype(BF16)
        right = jnp.concatenate([cotf_ref[h, rows, :] for h in range(2)], axis=1).astype(BF16)
        out = lax.dot_general(left, right, T0, preferred_element_type=F32)
        for h in range(2):
            jf_ref[h, pl.ds(s, 256, stride=8), :] = out[:, 128 * h : 128 * h + 128]
    low = iota((NY, NX, 8, 128), 2) < 4

    def step(z, carry):
        for h in range(2):
            t = jf_ref[h, pl.ds(z * 256, 256), :].reshape(NY, NK, NX, 8, 128)
            send_refs[h][z] = jnp.where(low, t[:, 0], pltpu.roll(t[:, 1], 4, 2)).astype(BF16)
        return carry

    lax.fori_loop(0, NZ, step, 0)


def core_sum(full_ref, core):
    def add(z, total):
        return total + jnp.sum(full_ref[z, :, core].reshape(NY * NX, 8, 128).astype(F32), axis=0)

    return lax.fori_loop(0, NZ, add, jnp.zeros((8, 128), F32))


def center(full_refs, totals, xc_ref, xn_ref):
    for h in range(2):
        total = totals[h]
        means = [jnp.sum(total[4 * k : 4 * k + 4], axis=0, keepdims=True) / N_S for k in range(2)]
        mean = jnp.where(iota((8, 128), 0) < 4, means[0], means[1])

        def step(z, carry):
            t = full_refs[h][z].reshape(32, 8, 128).astype(F32) - mean[None]
            t = t.astype(BF16).astype(F32)
            xc_ref[h, pl.ds(z * 32, 32)] = t
            t = t.reshape(16, 2, 8, 128)
            low = iota((16, 8, 128), 1) < 4
            one = jnp.where(low, t[:, 0], pltpu.roll(t[:, 1], 4, 1))
            two = jnp.where(low, pltpu.roll(t[:, 0], 4, 1), t[:, 1])
            for k, v in enumerate((one, two)):
                v = v.reshape(128, 128)
                xn_ref[k, pl.ds(z * 128, 128), 128 * h : 128 * h + 128] = v.astype(BF16)
            return carry

        lax.fori_loop(0, NZ, step, 0)


def gram_rows(owner_ref, core, xc_ref, left_ref):
    low = iota((8, 128), 0) < 4

    def step(i, carry):
        for j in range(16):
            q = i * 16 + j
            own = owner_ref[i * (2 * NK * NX * 2) + (j // NX) * (NK * NX) + core * NX + j % NX]
            for h in range(2):
                t = xc_ref[h, own]
                r = pltpu.roll(t, 4, 0)
                left_ref[0, q, :, 128 * h : 128 * h + 128] = jnp.where(low, t, r)
                left_ref[1, q, :, 128 * h : 128 * h + 128] = jnp.where(low, r, t)
        return carry

    lax.fori_loop(0, NZ, step, 0)


def gram_part(left_ref, xn_ref, out_ref, c):
    low = lax.rem(lax.div(iota((N_S, 256), 0), 4), 2) == 0
    rows = [left_ref[k].reshape(N_S, 256).astype(BF16) for k in range(2)]
    both = []
    for first in (256 * c, 256 * c + 512):
        out = None
        for k in range(2):
            part = lax.dot_general(rows[k], xn_ref[k, first : first + 256, :], NT, preferred_element_type=F32)
            out = part if out is None else out + part
        both.append(out)
    out = jnp.where(low, both[0], both[1]) * (1.0 / N_S)
    out_ref[...] = out.astype(BF16).reshape(NZ, NY, NX, 8, 256)


def add_outer(own, got_ref, out_ref, at, size):
    def step(z, carry):
        total = own(z).astype(F32)
        for off in range(1, size):
            total = total + got_ref[lax.rem(at + off, size), z].astype(F32)
        out_ref[z] = total.astype(BF16)
        return carry

    lax.fori_loop(0, NZ, step, 0)


def add_inner(own, got_ref, at, size):
    total = own.astype(F32)
    for off in range(1, size):
        total = total + got_ref[lax.rem(at + off, size)].astype(F32)
    return total


def own_info(index_ref, sign_ref, occ_ref, amp):
    sub, lane = iota((4, 128), 0), iota((4, 128), 1)
    pick = jnp.where(iota((32, 128), 0) == lax.div(iota((32, 128), 1), 4), 1.0, 0.0).astype(BF16)
    mine = sub == lax.rem(lane, 4)

    def row(v):
        v = jnp.dot(v.astype(F32).astype(BF16), pick, preferred_element_type=F32)
        return jnp.sum(jnp.where(mine, v, 0.0), axis=0, keepdims=True)

    index = index_ref[...]
    rows = [row(lax.shift_right_logical(index, 5)), row(jnp.bitwise_and(index, 31)), row(2 * sign_ref[...] - 1)]
    whole = jnp.sum(jnp.where(iota((8, 128), 0) == lax.rem(iota((8, 128), 1), 4), amp, 0.0), axis=0, keepdims=True)
    for _ in range(3):
        part = whole.astype(BF16).astype(F32)
        rows.append(part)
        whole = whole - part
    site = jnp.zeros((1, 128), F32)
    for i in range(4):
        o = occ_ref[i].astype(F32) - 0.5
        value = 4.0 * jnp.sum(o[0:1, :] * o[1:2, :], axis=1, keepdims=True)
        site = jnp.where(lax.rem(iota((1, 128), 1), 4) == i, value, site)
    rows += [site, jnp.zeros((1, 128), F32)]
    return jnp.concatenate(rows, axis=0).astype(BF16)


def kernel(
    owner_hbm, occ_s_hbm, occ_u_hbm, index_hbm, sign_hbm, embed_hbm, k_hbm, w_hbm, b_hbm, ro_hbm,
    energy_hbm, gram_hbm, force_hbm,
    owner_ref, energy_ref, gram_ref, force_ref, occ_s_ref, occ_u_ref, index_ref, sign_ref, embed_ref, k_ref, w_ref, b_ref, ro_ref,
    spread, wz, zs, zu, ss, su, kb, mix, sums, mixf, cotf, jf, xc, xn, left, uv, dense, part,
    a0, a1, a2, b0, b1, b2, fa, fb, ag, agf,
    ga, gb, ra1, rb1, ga2, gb2, ra2, rb2, ga3, gb3, ra3, rb3,
    ar_one, ar_two,
    send, recv, near,
):
    wire = Wire(send, recv)
    mz, my, mk, mx = (wire.at[a] for a in "zykx")
    fetched = [
        pltpu.make_async_copy(src, dst, near.at[i])
        for i, (src, dst) in enumerate(
            (
                (k_hbm, k_ref), (embed_hbm, embed_ref), (occ_s_hbm, occ_s_ref), (b_hbm, b_ref), (ro_hbm, ro_ref),
                (w_hbm, w_ref), (occ_u_hbm, occ_u_ref), (index_hbm, index_ref), (sign_hbm, sign_ref), (owner_hbm, owner_ref),
            )
        )
    ]
    for copy in fetched:
        copy.start()
    entry, count = wire.greet()
    spread_table(spread)
    for copy in fetched[:6]:
        copy.wait()
    for t in range(25):
        kb[t] = jnp.broadcast_to(k_ref[t, 1:2, :], (8, 256))
    tap_weights(embed_ref, k_ref, wz)

    patch_rows(occupied(occ_s_ref, 0, spread, 12, True), zs, 12)
    first_layer(zs, wz, w_ref, b_ref, ss, 0, 8)
    halo(ss, 8, True)

    def keep_mixed(x, mixed):
        for h in range(2):
            mixf[h, pl.ds(x * 128, 128), :] = mixed[:, 128 * h : 128 * h + 128].astype(BF16).astype(F32)

    def keep_cot(x, pre, th, out):
        g = 0.5 + 0.5 * th
        cot = ro_ref[...] * (1.0 - out * out) * (g * (1.0 + pre * (1.0 - g)))
        for h in range(2):
            cotf[h, pl.ds(x * 128, 128), :] = cot[:, 128 * h : 128 * h + 128].astype(BF16).astype(F32)

    SecondLayer(ss, kb, mix, w_ref, b_ref, sums, 8, keep_mixed, keep_cot).part(0, 8)
    jacobian(mixf, cotf, jf, (a0, b0))
    for copy in fetched[6:]:
        copy.wait()
    pl.semaphore_wait(entry, count)

    go_a = wire.start("z", lambda p: a0.at[p], lambda p: a1.at[p])
    go_b = wire.start("y", lambda p: b0.at[:, p], lambda p: b1.at[:, p])
    amp = jnp.broadcast_to(jnp.sum(sums[...] * ro_ref[...], axis=1, keepdims=True), (8, 128))
    amp = amp + pltpu.roll(amp, 4, 0)
    ag[mz, my, mk, mx] = own_info(index_ref, sign_ref, occ_s_ref, amp)
    go_i = wire.start("z", lambda p: ag.at[mz, my, mk, mx], lambda p: ag.at[p, my, mk, mx])
    a1[mz] = a0[mz]
    b1[:, my] = b0[:, my]

    layer = SecondLayer(su, kb, mix, w_ref, b_ref, sums, 16)

    def unique():
        for g in range(4):
            patch_rows(occupied(occ_u_ref, 8 * g, spread, 20, False), zu, 20)
            yield
            first_layer(zu, wz, w_ref, b_ref, su, 0, 8)
            yield
            first_layer(zu, wz, w_ref, b_ref, su, 8, 16)
            halo(su, 16, False)
            yield
            for x in range(0, 16, 4):
                layer.part(x, x + 4)
                if x == 12:
                    uv[8 * g : 8 * g + 8, :] = jnp.broadcast_to(
                        jnp.sum(sums[...] * ro_ref[...], axis=1, keepdims=True), (8, 128)
                    )
                yield

    pieces = unique()

    def work(n):
        for _ in range(n):
            next(pieces, None)

    work(WORK[0])
    wait(go_b, go_i)
    go_b = wire.start("x", lambda p: b1.at[:, :, p], lambda p: b2.at[:, :, p])
    go_i = wire.start("x", lambda p: ag.at[:, my, mk, mx], lambda p: ag.at[:, my, mk, p])
    b2[:, :, mx] = b1[:, :, mx]
    work(WORK[1])
    wait(go_a)
    go_a = wire.start("y", lambda p: a1.at[:, p], lambda p: a2.at[:, p])
    a2[:, my] = a1[:, my]
    work(WORK[2])
    wait(go_b, go_i)
    go_b = wire.start("z", lambda p: b2.at[p], lambda p: fb.at[p, :, mk])
    fb[mz, :, mk] = b2[mz]
    work(WORK[3])
    wait(go_a)
    go_a = wire.start("x", lambda p: a2.at[:, :, p], lambda p: fa.at[:, :, mk, p])
    go_i = wire.start("y", lambda p: ag.at[:, my, mk], lambda p: ag.at[:, p, mk])
    fa[:, :, mk, mx] = a2[:, :, mx]
    work(WORK[4])
    wait(go_a)
    go_a = wire.start("k", lambda p: fa.at[:, :, mk], lambda p: fa.at[:, :, p])
    wait(go_b)
    go_b = wire.start("k", lambda p: fb.at[:, :, mk], lambda p: fb.at[:, :, p])
    totals = [core_sum(full, mk) for full in (fa, fb)]
    work(WORK[5])
    wait(go_i, go_a, go_b)
    go_i = wire.start("k", lambda p: ag.at[:, :, mk], lambda p: ag.at[:, :, p])

    totals = [total + core_sum(full, 1 - mk) for total, full in zip(totals, (fa, fb))]
    center((fa, fb), totals, xc, xn)
    gram_rows(owner_ref, mk, xc, left)
    gram_part(left, xn, ga, 0)
    go_a = wire.start("x", lambda p: ga.at[:, :, p], lambda p: ra1.at[p])
    gram_part(left, xn, gb, 1)
    go_b = wire.start("y", lambda p: gb.at[:, p], lambda p: rb1.at[p])
    wait(go_i)

    def widen(z, carry):
        agf[pl.ds(z * 256, 256), :] = ag[z].reshape(256, 128).astype(F32)
        return carry

    lax.fori_loop(0, NZ, widen, 0)
    for r in range(8):
        rows = pl.ds(32 * r, 32)
        v = [agf[pl.ds(256 * r + row, 32, stride=8), :] for row in range(7)]
        dense[0, rows, :] = v[0]
        dense[1, rows, :] = v[1]
        dense[2, rows, :] = v[2]
        dense[3, rows, :] = v[3] + v[4] + v[5]
        dense[4, rows, :] = v[6]
    work(28)

    mine = wire.linear().astype(F32)
    place = iota((32, 128), 0) == lax.div(iota((32, 128), 1), 4)
    hop, site = [], []
    for r in range(8):
        rows = pl.ds(32 * r, 32)
        local = dense[1, rows, :]
        pick = jnp.zeros((32, 128), F32)
        for u in range(32):
            pick = jnp.where(local == u, uv[u : u + 1, :], pick)
        known = dense[0, rows, :] == mine
        value = jnp.where(known, pick - dense[3, rows, :], 0.0)
        value = jnp.where(known, dense[2, rows, :] * jnp.exp(value), 0.0)
        for shift in (4, 8, 16, 32, 64):
            value = value + pltpu.roll(value, shift, 1)
        hop.append(jnp.sum(jnp.where(place, value, 0.0), axis=0, keepdims=True))
        site.append(jnp.sum(jnp.where(place, dense[4, rows, :], 0.0), axis=0, keepdims=True))
    part[0] = jnp.concatenate(hop, axis=0)
    go_e = wire.share(PLANES[0], part.at[0], ar_one)

    wait(go_a, go_b)
    add_outer(lambda z: ga[z, :, mx], ra1, ga2, mx, NX)
    add_outer(lambda z: gb[z, my], rb1, gb2, my, NY)
    go_a = wire.start("y", lambda p: ga2.at[:, p], lambda p: ra2.at[p])
    go_b = wire.start("x", lambda p: gb2.at[:, p], lambda p: rb2.at[p])
    wait(go_e)
    part[1] = add_inner(part[0], ar_one, wire.rank(PLANES[0]), NZ * NK)
    go_e = wire.share(PLANES[1], part.at[1], ar_two)
    wait(go_a, go_b)
    ga3[...] = add_inner(ga2[:, my], ra2, my, NY).astype(BF16)
    gb3[...] = add_inner(gb2[:, mx], rb2, mx, NX).astype(BF16)
    go_a = wire.start("z", lambda p: ga3.at[p], lambda p: ra3.at[p])
    go_b = wire.start("z", lambda p: gb3.at[p], lambda p: rb3.at[p])
    wait(go_e)
    hopping = add_inner(part[1], ar_two, wire.rank(PLANES[1]), NY * NX)
    energy = jnp.concatenate(site, axis=0) - hopping
    own = jnp.where(iota((8, 128), 0) == lax.div(wire.linear(), 32), energy, 0.0)
    own = jnp.broadcast_to(jnp.sum(own, axis=0, keepdims=True), (8, 128))
    own = pltpu.roll(own, lax.rem(128 - 4 * lax.rem(wire.linear(), 32), 128), 1)
    energy_ref[...] = own[0:1, 0:4]
    leave = [pltpu.make_async_copy(energy_ref, energy_hbm, near.at[0])]
    leave[0].start()
    shifted = energy - jnp.sum(energy) / N_S
    high = shifted.astype(BF16)
    rest = shifted - high.astype(F32)
    middle = rest.astype(BF16)
    low = (rest - middle.astype(F32)).astype(BF16)
    three = jnp.concatenate([high, middle, low], axis=0)
    force = jnp.zeros((8, 256), F32)
    for r in range(8):
        out = jnp.dot(three, xn[mk, pl.ds(128 * r, 128), :], preferred_element_type=F32)
        out = out[0:8] + out[8:16] + out[16:24]
        force = force + jnp.where(iota((8, 256), 0) == r, out, 0.0)
    force_ref[...] = jnp.sum(force, axis=0, keepdims=True) / N_S
    leave.append(pltpu.make_async_copy(force_ref, force_hbm, near.at[1]))
    leave[1].start()

    wait(go_a, go_b)
    one = add_inner(ga3[mz], ra3, mz, NZ)
    two = add_inner(gb3[mz], rb3, mz, NZ)
    for h in range(2):
        gram_ref[:, 512 * h : 512 * h + 256] = one[4 * h : 4 * h + 4]
        gram_ref[:, 512 * h + 256 : 512 * h + 512] = two[4 * h : 4 * h + 4]
    leave.append(pltpu.make_async_copy(gram_ref, gram_hbm, near.at[2]))
    leave[2].start()
    wait(*leave)


def deliver(*refs):
    copies = [pltpu.make_async_copy(refs[i], refs[3 + i], refs[6].at[i]) for i in range(3)]
    for copy in copies:
        copy.start()
    wait(*copies)


def body(sample_occ, unique_occ, conn_index, hop_sign, gram_owner, embed, kernels, weights, biases, readout):
    grid = (NZ, NY, NX, 8, 128)
    operands = (
        sample_occ, unique_occ, conn_index, hop_sign, embed, kernels.transpose(1, 0, 2),
        weights, biases, readout.reshape(1, 256),
    )
    results = (
        jax.ShapeDtypeStruct((1, 4), F32),
        jax.ShapeDtypeStruct((4, N_S), F32),
        jax.ShapeDtypeStruct((1, 256), F32),
    )
    made = pl.pallas_call(
        kernel,
        out_shape=results,
        in_specs=[pl.BlockSpec(memory_space=pl.ANY)] * 10,
        out_specs=(pl.BlockSpec(memory_space=pl.ANY),) * 3,
        scratch_shapes=[
            pltpu.SMEM((256,), jnp.int32),
            pltpu.VMEM((1, 4), F32),
            pltpu.VMEM((4, N_S), F32),
            pltpu.VMEM((1, 256), F32),
        ]
        + [pltpu.VMEM(v.shape, v.dtype) for v in operands]
        + [
            pltpu.VMEM((8, 256, 128), BF16),
            pltpu.VMEM((160, 512), BF16),
            pltpu.VMEM((12, 16, 128), F32),
            pltpu.VMEM((20, 16, 128), F32),
            pltpu.VMEM((12, 16, 8, 256), F32),
            pltpu.VMEM((20, 16, 8, 256), F32),
            pltpu.VMEM((25, 8, 256), F32),
            pltpu.VMEM((2, 128, 256), BF16),
            pltpu.VMEM((8, 256), F32),
            pltpu.VMEM((2, 1024, 128), F32),
            pltpu.VMEM((2, 1024, 128), F32),
            pltpu.VMEM((2, 2048, 128), F32),
            pltpu.VMEM((2, 256, 8, 128), F32),
            pltpu.VMEM((2, 1024, 256), BF16),
            pltpu.VMEM((2, 128, 8, 256), F32),
            pltpu.VMEM((32, 128), F32),
            pltpu.VMEM((5, 256, 128), F32),
            pltpu.VMEM((2, 8, 128), F32),
        ]
        + [pltpu.VMEM(grid, BF16)] * 6
        + [pltpu.VMEM((NZ, NY, NK, NX, 8, 128), BF16)] * 3
        + [pltpu.VMEM((2048, 128), F32)]
        + [pltpu.VMEM((NZ, NY, NX, 8, 256), BF16)] * 2
        + [pltpu.VMEM((4, NZ, 4, 8, 256), BF16)] * 2
        + [pltpu.VMEM((NZ, 4, 8, 256), BF16)] * 2
        + [pltpu.VMEM((4, NZ, 8, 256), BF16)] * 2
        + [pltpu.VMEM((NZ, 8, 256), BF16)] * 4
        + [pltpu.VMEM((16, 8, 128), F32)] * 2
        + [pltpu.SemaphoreType.DMA((n,)) for n in (20, 20, 10)],
        compiler_params=pltpu.CompilerParams(
            collective_id=0, has_side_effects=True, vmem_limit_bytes=60 << 20
        ),
        name="local_energy_gram",
    )(gram_owner, *operands)
    energy, gram, force = pl.pallas_call(
        deliver,
        out_shape=results,
        in_specs=[pl.BlockSpec(memory_space=pl.ANY)] * 3,
        out_specs=(pl.BlockSpec(memory_space=pl.ANY),) * 3,
        scratch_shapes=[pltpu.SemaphoreType.DMA((3,))],
        name="deliver",
    )(*made)
    return energy.reshape(4), gram, force.reshape(256)


def solution(mesh):
    both = ("eval", "blk")
    return jax.shard_map(
        body,
        mesh=mesh,
        in_specs=(P(both), P(both), P(both), P(both), P(), P(), P(), P(), P(), P()),
        out_specs=(P(both), P(both), P(both)),
        check_vma=False,
    )
```

```python
import jax
import jax.numpy as jnp
from jax import lax
from jax.experimental import pallas as pl
from jax.experimental.pallas import tpu as pltpu
from jax.sharding import PartitionSpec as P

MESH = pl.DeviceIdType.MESH
PLANES = (("z", "k"), ("y", "x"))
F32 = jnp.float32
BF16 = jnp.bfloat16
NZ, NY, NX, NK = 8, 4, 4, 2
N_S = 1024
WORK = (8, 3, 3, 3, 6, 1)
T0 = (((0,), (0,)), ((), ()))
NT = (((1,), (1,)), ((), ()))


def iota(shape, dim):
    return lax.broadcasted_iota(jnp.int32, shape, dim)


def spread_table(spread_ref):
    site, lane = iota((256, 128), 0), iota((256, 128), 1)
    same = lax.rem(site, 16) == lax.div(lane, 8)
    for c in range(8):
        hit = jnp.logical_and(same, lax.rem(lane, 8) == c)
        spread_ref[c] = jnp.where(hit, 1.0, 0.0).astype(BF16)


def occupied(occ_ref, first, spread_ref, rows, split):
    total = None
    sub, lane = iota((1, 8, 256), 1), iota((rows, 8, 256), 2)
    for c in range(8):
        o = occ_ref[first + (c % 4 if split else c)].astype(F32)
        o = jnp.where(lax.rem(sub, 2) == 0, o[0:1, :][None], o[1:2, :][None])
        row = lax.rem(iota((rows, 8, 256), 0) + (14 + (8 * (c // 4) if split else 0)), 16)
        o = jnp.where(lax.div(lane, 16) == row, o, 0.0).reshape(rows * 8, 256).astype(BF16)
        part = jnp.dot(o, spread_ref[c], preferred_element_type=F32)
        total = part if total is None else total + part
    return total.reshape(rows, 8, 128)


def patch_rows(t, zed_ref, rows):
    sub = iota((rows, 8, 128), 1)
    r = [t if dy == 2 else pltpu.roll(t, (8 * (2 - dy)) % 128, 2) for dy in range(5)]
    first = jnp.where(sub < 2, r[0], jnp.where(sub < 4, r[1], jnp.where(sub < 6, r[2], r[3])))
    second = jnp.where(sub < 2, r[4], jnp.where(sub == 2, 1.0, 0.0))
    zed_ref[:, 0:8, :] = first
    zed_ref[:, 8:16, :] = second


def tap_weights(embed_ref, k_ref, wz_ref):
    sub = iota((8, 256), 0)
    spin = jnp.where(lax.rem(sub, 2) == 0, embed_ref[0:1, :], embed_ref[1:2, :])
    const = embed_ref[2:3, :] * jnp.sum(k_ref[...], axis=0)[0:1, :]
    for dx in range(5):
        k = [k_ref[dx * 5 + dy, 0:1, :] for dy in range(5)]
        top = jnp.where(sub < 2, k[0], jnp.where(sub < 4, k[1], jnp.where(sub < 6, k[2], k[3]))) * spin
        low = jnp.where(sub < 2, k[4] * spin, jnp.where(sub == 2, const, 0.0) if dx == 0 else 0.0)
        own = jnp.where(lax.div(sub, 2) == 2, spin, 0.0) if dx == 2 else jnp.zeros((8, 256), F32)
        one = jnp.where(sub == 2, embed_ref[2:3, :], 0.0) if dx == 0 else jnp.zeros((8, 256), F32)
        base = jnp.concatenate(
            [jnp.concatenate([top, low], axis=0), jnp.concatenate([own, one], axis=0)], axis=1
        )
        high = base.astype(BF16)
        wz_ref[16 * dx : 16 * dx + 16, :] = high
        wz_ref[80 + 16 * dx : 96 + 16 * dx, :] = (base - high.astype(F32)).astype(BF16)


def first_layer(zed_ref, wz_ref, w_ref, b_ref, state_ref, low, high):
    many = 4

    def step(i, carry):
        xs = [i * many + k for k in range(many)]
        cols = []
        for x in xs:
            taps = [zed_ref[x + j].astype(BF16) for j in range(5)]
            cols.append(jnp.concatenate(taps + taps, axis=0))
        cols = jnp.concatenate(cols, axis=1)
        both = lax.dot_general(cols, wz_ref[...], T0, preferred_element_type=F32)
        mixed = both[:, :256].astype(BF16)
        pre = jnp.dot(mixed, w_ref[0], preferred_element_type=F32) + b_ref[0:1, :]
        half = 0.5 * pre
        new = both[:, 256:] + (half + half * jnp.tanh(half))
        state_ref[pl.ds(i * many + 2, many)] = new.reshape(many, 16, 8, 256)
        return carry

    lax.fori_loop(low // many, high // many, step, 0)


def halo(state_ref, rows, swap):
    for i in (0, 1):
        low = state_ref[rows + i]
        high = state_ref[2 + i]
        if swap:
            low = pltpu.roll(low, 4, 1)
            high = pltpu.roll(high, 4, 1)
        state_ref[i] = low
        state_ref[rows + 2 + i] = high


def convolve(state_ref, kb_ref, x):
    halves = []
    for h in range(2):
        lanes = slice(128 * h, 128 * h + 128)
        acc = None
        for dx in range(5):
            row = state_ref[x + dx, :, :, lanes]
            for dy in range(5):
                s = (dy - 2) % 16
                moved = row if s == 0 else jnp.concatenate([row[s:], row[:s]], axis=0)
                term = moved * kb_ref[dx * 5 + dy, :, lanes][None]
                acc = term if acc is None else acc + term
        halves.append(acc.reshape(128, 128))
    return jnp.concatenate(halves, axis=1)


class SecondLayer:
    def __init__(self, state_ref, kb_ref, mix_ref, w_ref, b_ref, total_ref, rows, keep_mixed=None, keep_rest=None):
        self.state, self.kb, self.mix, self.w, self.b = state_ref, kb_ref, mix_ref, w_ref, b_ref
        self.total, self.rows, self.keep_mixed, self.keep_rest = total_ref, rows, keep_mixed, keep_rest

    def finish(self, x, total):
        pre = jnp.dot(self.mix[lax.rem(x, 2)], self.w[1], preferred_element_type=F32) + self.b[1:2, :]
        half = 0.5 * pre
        th_half = jnp.tanh(half)
        out = jnp.tanh(self.state[x + 2].reshape(128, 256) + (half + half * th_half))
        if self.keep_rest is not None:
            self.keep_rest(x, pre, th_half, out)
        return total + jnp.sum(out.reshape(16, 8, 256), axis=0)

    def make(self, x):
        mixed = convolve(self.state, self.kb, x)
        self.mix[lax.rem(x, 2)] = mixed.astype(BF16)
        if self.keep_mixed is not None:
            self.keep_mixed(x, mixed)

    def part(self, low, high):
        if low == 0:
            self.make(jnp.int32(0))
            self.total[...] = jnp.zeros((8, 256), F32)

        def step(x, total):
            total = self.finish(x - 1, total)
            self.make(x)
            return total

        total = lax.fori_loop(max(low, 1), high, step, self.total[...])
        self.total[...] = self.finish(jnp.int32(high - 1), total) if high == self.rows else total


class Wire:
    def __init__(self, send, recv):
        e, x = lax.axis_index("eval"), lax.axis_index("blk")
        self.at = {
            "z": lax.div(e, NY * NK),
            "y": lax.rem(lax.div(e, NK), NY),
            "k": lax.rem(e, NK),
            "x": x,
        }
        self.size = {"z": NZ, "y": NY, "k": NK, "x": NX}
        self.send, self.recv, self.used = send, recv, 0

    def linear(self):
        return ((self.at["z"] * NY + self.at["y"]) * NK + self.at["k"]) * NX + self.at["x"]

    def peer(self, axis, off):
        return lax.rem(self.at[axis] + off, self.size[axis])

    def device(self, axis, place):
        at = {**self.at, axis: place}
        return ((at["z"] * NY + at["y"]) * NK + at["k"], at["x"])

    def member(self, axes, place):
        inner = self.size[axes[1]]
        at = {**self.at, axes[0]: lax.div(place, inner), axes[1]: lax.rem(place, inner)}
        return ((at["z"] * NY + at["y"]) * NK + at["k"], at["x"])

    def rank(self, axes):
        return self.at[axes[0]] * self.size[axes[1]] + self.at[axes[1]]

    def greet(self):
        sem = pltpu.get_barrier_semaphore()
        count = 0
        for axes in PLANES:
            many = self.size[axes[0]] * self.size[axes[1]]
            for off in range(1, many):
                place = lax.rem(self.rank(axes) + off, many)
                pl.semaphore_signal(sem, inc=1, device_id=self.member(axes, place), device_id_type=MESH)
                count += 1
        return sem, count

    def pair(self):
        self.used += 1
        return {"send_sem": self.send.at[self.used - 1], "recv_sem": self.recv.at[self.used - 1]}

    def end(self, sems, region, device):
        return pltpu.make_async_remote_copy(
            src_ref=region, dst_ref=region, device_id=device, device_id_type=MESH, **sems
        )

    def share(self, axes, src, dst_ref):
        many = self.size[axes[0]] * self.size[axes[1]]
        sems = self.pair()
        for off in range(1, many):
            device = self.member(axes, lax.rem(self.rank(axes) + off, many))
            pltpu.make_async_remote_copy(
                src_ref=src, dst_ref=dst_ref.at[self.rank(axes)], device_id=device, device_id_type=MESH, **sems
            ).start()
        return self.end(sems, dst_ref.at[0 : many - 1], device)

    def push(self, axis, src, dst, sems):
        for off in range(1, self.size[axis]):
            place = self.peer(axis, off)
            pltpu.make_async_remote_copy(
                src_ref=src(place),
                dst_ref=dst(self.at[axis]),
                device_id=self.device(axis, place),
                device_id_type=MESH,
                **sems,
            ).start()

    def start(self, axis, src, dst):
        sems = self.pair()
        self.push(axis, src, dst, sems)
        return self.end(sems, dst(pl.ds(0, self.size[axis] - 1)), self.device(axis, self.peer(axis, 1)))


def wait(*groups):
    for group in groups:
        group.wait()


def jacobian(mixf_ref, cotf_ref, jf_ref):
    for s in range(4):
        rows = pl.ds(s, 256, stride=4)
        left = jnp.concatenate([mixf_ref[h, rows, :] for h in range(2)], axis=1).astype(BF16)
        right = jnp.concatenate([cotf_ref[h, rows, :] for h in range(2)], axis=1).astype(BF16)
        out = lax.dot_general(left, right, T0, preferred_element_type=F32)
        for h in range(2):
            jf_ref[h, pl.ds(s, 256, stride=8), :] = out[:, 128 * h : 128 * h + 128]


def lay_out(jf_ref, h, send_ref):
    low = iota((NY, NX, 8, 128), 2) < 4
    for z in range(NZ):
        t = jf_ref[h, z * 256 : z * 256 + 256, :].reshape(NY, NK, NX, 8, 128)
        send_ref[z] = jnp.where(low, t[:, 0], pltpu.roll(t[:, 1], 4, 2)).astype(BF16)


def core_sum(full_ref, core):
    def add(z, total):
        return total + jnp.sum(full_ref[z, :, core].reshape(NY * NX, 8, 128).astype(F32), axis=0)

    return lax.fori_loop(0, NZ, add, jnp.zeros((8, 128), F32))


def center(full_refs, totals, xc_ref, xn_ref):
    for h in range(2):
        total = totals[h]
        means = [jnp.sum(total[4 * k : 4 * k + 4], axis=0, keepdims=True) / N_S for k in range(2)]
        mean = jnp.where(iota((8, 128), 0) < 4, means[0], means[1])

        def step(z, carry):
            t = full_refs[h][z].reshape(32, 8, 128).astype(F32) - mean[None]
            t = t.astype(BF16).astype(F32)
            xc_ref[h, pl.ds(z * 32, 32)] = t
            t = t.reshape(16, 2, 8, 128)
            low = iota((16, 8, 128), 1) < 4
            one = jnp.where(low, t[:, 0], pltpu.roll(t[:, 1], 4, 1))
            two = jnp.where(low, pltpu.roll(t[:, 0], 4, 1), t[:, 1])
            for k, v in enumerate((one, two)):
                v = v.reshape(128, 128)
                xn_ref[k, pl.ds(z * 128, 128), 128 * h : 128 * h + 128] = v.astype(BF16)
            return carry

        lax.fori_loop(0, NZ, step, 0)


def gram_rows(owner_ref, core, xc_ref, left_ref):
    low = iota((8, 128), 0) < 4

    def step(i, carry):
        for j in range(16):
            q = i * 16 + j
            own = owner_ref[i * (2 * NK * NX * 2) + (j // NX) * (NK * NX) + core * NX + j % NX]
            for h in range(2):
                t = xc_ref[h, own]
                r = pltpu.roll(t, 4, 0)
                left_ref[0, q, :, 128 * h : 128 * h + 128] = jnp.where(low, t, r)
                left_ref[1, q, :, 128 * h : 128 * h + 128] = jnp.where(low, r, t)
        return carry

    lax.fori_loop(0, NZ, step, 0)


def gram_part(left_ref, xn_ref, out_ref, c):
    low = lax.rem(lax.div(iota((N_S, 256), 0), 4), 2) == 0
    rows = [left_ref[k].reshape(N_S, 256).astype(BF16) for k in range(2)]
    both = []
    for first in (256 * c, 256 * c + 512):
        out = None
        for k in range(2):
            part = lax.dot_general(rows[k], xn_ref[k, first : first + 256, :], NT, preferred_element_type=F32)
            out = part if out is None else out + part
        both.append(out)
    out = jnp.where(low, both[0], both[1]) * (1.0 / N_S)
    out_ref[...] = out.astype(BF16).reshape(NZ, NY, NX, 8, 256)


def add_outer(own, got_ref, out_ref, at, size):
    def step(z, carry):
        total = own(z).astype(F32)
        for off in range(1, size):
            total = total + got_ref[lax.rem(at + off, size), z].astype(F32)
        out_ref[z] = total.astype(BF16)
        return carry

    lax.fori_loop(0, NZ, step, 0)


def add_inner(own, got_ref, at, size):
    total = own.astype(F32)
    for off in range(1, size):
        total = total + got_ref[lax.rem(at + off, size)].astype(F32)
    return total


def own_info(index_ref, sign_ref, occ_ref, amp):
    sub, lane = iota((4, 128), 0), iota((4, 128), 1)
    pick = jnp.where(iota((32, 128), 0) == lax.div(iota((32, 128), 1), 4), 1.0, 0.0).astype(BF16)
    mine = sub == lax.rem(lane, 4)

    def row(v):
        v = jnp.dot(v.astype(F32).astype(BF16), pick, preferred_element_type=F32)
        return jnp.sum(jnp.where(mine, v, 0.0), axis=0, keepdims=True)

    index = index_ref[...]
    rows = [row(lax.shift_right_logical(index, 5)), row(jnp.bitwise_and(index, 31)), row(2 * sign_ref[...] - 1)]
    whole = jnp.sum(jnp.where(iota((8, 128), 0) == lax.rem(iota((8, 128), 1), 4), amp, 0.0), axis=0, keepdims=True)
    for _ in range(3):
        part = whole.astype(BF16).astype(F32)
        rows.append(part)
        whole = whole - part
    site = jnp.zeros((1, 128), F32)
    for i in range(4):
        o = occ_ref[i].astype(F32) - 0.5
        value = 4.0 * jnp.sum(o[0:1, :] * o[1:2, :], axis=1, keepdims=True)
        site = jnp.where(lax.rem(iota((1, 128), 1), 4) == i, value, site)
    rows += [site, jnp.zeros((1, 128), F32)]
    return jnp.concatenate(rows, axis=0).astype(BF16)


def kernel(
    owner_hbm, occ_s_hbm, occ_u_hbm, index_hbm, sign_hbm, embed_hbm, k_hbm, w_hbm, b_hbm, ro_hbm,
    energy_hbm, gram_hbm, force_hbm,
    owner_ref, energy_ref, gram_ref, force_ref, occ_s_ref, occ_u_ref, index_ref, sign_ref, embed_ref, k_ref, w_ref, b_ref, ro_ref,
    spread, wz, zs, zu, ss, su, kb, mix, sums, mixf, cotf, jf, xc, xn, left, uv, dense, part,
    a0, a1, a2, b0, b1, b2, fa, fb, ag, agf,
    ga, gb, ra1, rb1, ga2, gb2, ra2, rb2, ga3, gb3, ra3, rb3,
    ar_one, ar_two,
    send, recv, near,
):
    wire = Wire(send, recv)
    mz, my, mk, mx = (wire.at[a] for a in "zykx")
    fetched = [
        pltpu.make_async_copy(src, dst, near.at[i])
        for i, (src, dst) in enumerate(
            (
                (k_hbm, k_ref), (embed_hbm, embed_ref), (occ_s_hbm, occ_s_ref), (b_hbm, b_ref), (ro_hbm, ro_ref),
                (w_hbm, w_ref), (occ_u_hbm, occ_u_ref), (index_hbm, index_ref), (sign_hbm, sign_ref), (owner_hbm, owner_ref),
            )
        )
    ]
    for copy in fetched:
        copy.start()
    entry, count = wire.greet()
    spread_table(spread)
    for copy in fetched[:6]:
        copy.wait()
    for t in range(25):
        kb[t] = jnp.broadcast_to(k_ref[t, 1:2, :], (8, 256))
    tap_weights(embed_ref, k_ref, wz)

    patch_rows(occupied(occ_s_ref, 0, spread, 12, True), zs, 12)
    first_layer(zs, wz, w_ref, b_ref, ss, 0, 8)
    halo(ss, 8, True)

    def keep_mixed(x, mixed):
        for h in range(2):
            mixf[h, pl.ds(x * 128, 128), :] = mixed[:, 128 * h : 128 * h + 128].astype(BF16).astype(F32)

    def keep_cot(x, pre, th, out):
        g = 0.5 + 0.5 * th
        cot = ro_ref[...] * (1.0 - out * out) * (g * (1.0 + pre * (1.0 - g)))
        for h in range(2):
            cotf[h, pl.ds(x * 128, 128), :] = cot[:, 128 * h : 128 * h + 128].astype(BF16).astype(F32)

    SecondLayer(ss, kb, mix, w_ref, b_ref, sums, 8, keep_mixed, keep_cot).part(0, 8)
    jacobian(mixf, cotf, jf)
    lay_out(jf, 0, a0)
    for copy in fetched[6:]:
        copy.wait()
    pl.semaphore_wait(entry, count)

    go_a = wire.start("z", lambda p: a0.at[p], lambda p: a1.at[p])
    lay_out(jf, 1, b0)
    go_b = wire.start("y", lambda p: b0.at[:, p], lambda p: b1.at[:, p])
    amp = jnp.broadcast_to(jnp.sum(sums[...] * ro_ref[...], axis=1, keepdims=True), (8, 128))
    amp = amp + pltpu.roll(amp, 4, 0)
    ag[mz, my, mk, mx] = own_info(index_ref, sign_ref, occ_s_ref, amp)
    go_i = wire.start("z", lambda p: ag.at[mz, my, mk, mx], lambda p: ag.at[p, my, mk, mx])
    a1[mz] = a0[mz]
    b1[:, my] = b0[:, my]

    layer = SecondLayer(su, kb, mix, w_ref, b_ref, sums, 16)

    def unique():
        for g in range(4):
            patch_rows(occupied(occ_u_ref, 8 * g, spread, 20, False), zu, 20)
            yield
            first_layer(zu, wz, w_ref, b_ref, su, 0, 8)
            yield
            first_layer(zu, wz, w_ref, b_ref, su, 8, 16)
            halo(su, 16, False)
            yield
            for x in range(0, 16, 4):
                layer.part(x, x + 4)
                if x == 12:
                    uv[8 * g : 8 * g + 8, :] = jnp.broadcast_to(
                        jnp.sum(sums[...] * ro_ref[...], axis=1, keepdims=True), (8, 128)
                    )
                yield

    pieces = unique()

    def work(n):
        for _ in range(n):
            next(pieces, None)

    work(WORK[0])
    wait(go_b, go_i)
    go_b = wire.start("x", lambda p: b1.at[:, :, p], lambda p: b2.at[:, :, p])
    go_i = wire.start("x", lambda p: ag.at[:, my, mk, mx], lambda p: ag.at[:, my, mk, p])
    b2[:, :, mx] = b1[:, :, mx]
    work(WORK[1])
    wait(go_a)
    go_a = wire.start("y", lambda p: a1.at[:, p], lambda p: a2.at[:, p])
    a2[:, my] = a1[:, my]
    work(WORK[2])
    wait(go_b, go_i)
    go_b = wire.start("z", lambda p: b2.at[p], lambda p: fb.at[p, :, mk])
    fb[mz, :, mk] = b2[mz]
    work(WORK[3])
    wait(go_a)
    go_a = wire.start("x", lambda p: a2.at[:, :, p], lambda p: fa.at[:, :, mk, p])
    go_i = wire.start("y", lambda p: ag.at[:, my, mk], lambda p: ag.at[:, p, mk])
    fa[:, :, mk, mx] = a2[:, :, mx]
    work(WORK[4])
    wait(go_a)
    go_a = wire.start("k", lambda p: fa.at[:, :, mk], lambda p: fa.at[:, :, p])
    wait(go_b)
    go_b = wire.start("k", lambda p: fb.at[:, :, mk], lambda p: fb.at[:, :, p])
    totals = [core_sum(full, mk) for full in (fa, fb)]
    work(WORK[5])
    wait(go_i, go_a, go_b)
    go_i = wire.start("k", lambda p: ag.at[:, :, mk], lambda p: ag.at[:, :, p])

    totals = [total + core_sum(full, 1 - mk) for total, full in zip(totals, (fa, fb))]
    center((fa, fb), totals, xc, xn)
    gram_rows(owner_ref, mk, xc, left)
    gram_part(left, xn, ga, 0)
    go_a = wire.start("x", lambda p: ga.at[:, :, p], lambda p: ra1.at[p])
    gram_part(left, xn, gb, 1)
    go_b = wire.start("y", lambda p: gb.at[:, p], lambda p: rb1.at[p])
    wait(go_i)

    def widen(z, carry):
        agf[pl.ds(z * 256, 256), :] = ag[z].reshape(256, 128).astype(F32)
        return carry

    lax.fori_loop(0, NZ, widen, 0)
    for r in range(8):
        rows = pl.ds(32 * r, 32)
        v = [agf[pl.ds(256 * r + row, 32, stride=8), :] for row in range(7)]
        dense[0, rows, :] = v[0]
        dense[1, rows, :] = v[1]
        dense[2, rows, :] = v[2]
        dense[3, rows, :] = v[3] + v[4] + v[5]
        dense[4, rows, :] = v[6]
    work(28)

    mine = wire.linear().astype(F32)
    place = iota((32, 128), 0) == lax.div(iota((32, 128), 1), 4)
    hop, site = [], []
    for r in range(8):
        rows = pl.ds(32 * r, 32)
        local = dense[1, rows, :]
        pick = jnp.zeros((32, 128), F32)
        for u in range(32):
            pick = jnp.where(local == u, uv[u : u + 1, :], pick)
        known = dense[0, rows, :] == mine
        value = jnp.where(known, pick - dense[3, rows, :], 0.0)
        value = jnp.where(known, dense[2, rows, :] * jnp.exp(value), 0.0)
        for shift in (4, 8, 16, 32, 64):
            value = value + pltpu.roll(value, shift, 1)
        hop.append(jnp.sum(jnp.where(place, value, 0.0), axis=0, keepdims=True))
        site.append(jnp.sum(jnp.where(place, dense[4, rows, :], 0.0), axis=0, keepdims=True))
    part[0] = jnp.concatenate(hop, axis=0)
    go_e = wire.share(PLANES[0], part.at[0], ar_one)

    wait(go_a)
    add_outer(lambda z: ga[z, :, mx], ra1, ga2, mx, NX)
    go_a = wire.start("y", lambda p: ga2.at[:, p], lambda p: ra2.at[p])
    wait(go_b)
    add_outer(lambda z: gb[z, my], rb1, gb2, my, NY)
    go_b = wire.start("x", lambda p: gb2.at[:, p], lambda p: rb2.at[p])
    wait(go_e)
    part[1] = add_inner(part[0], ar_one, wire.rank(PLANES[0]), NZ * NK)
    go_e = wire.share(PLANES[1], part.at[1], ar_two)
    wait(go_a)
    ga3[...] = add_inner(ga2[:, my], ra2, my, NY).astype(BF16)
    go_a = wire.start("z", lambda p: ga3.at[p], lambda p: ra3.at[p])
    wait(go_b)
    gb3[...] = add_inner(gb2[:, mx], rb2, mx, NX).astype(BF16)
    go_b = wire.start("z", lambda p: gb3.at[p], lambda p: rb3.at[p])
    wait(go_e)
    hopping = add_inner(part[1], ar_two, wire.rank(PLANES[1]), NY * NX)
    energy = jnp.concatenate(site, axis=0) - hopping
    own = jnp.where(iota((8, 128), 0) == lax.div(wire.linear(), 32), energy, 0.0)
    own = jnp.broadcast_to(jnp.sum(own, axis=0, keepdims=True), (8, 128))
    own = pltpu.roll(own, lax.rem(128 - 4 * lax.rem(wire.linear(), 32), 128), 1)
    energy_ref[...] = own[0:1, 0:4]
    leave = [pltpu.make_async_copy(energy_ref, energy_hbm, near.at[0])]
    leave[0].start()
    shifted = energy - jnp.sum(energy) / N_S
    high = shifted.astype(BF16)
    rest = shifted - high.astype(F32)
    middle = rest.astype(BF16)
    low = (rest - middle.astype(F32)).astype(BF16)
    three = jnp.concatenate([high, middle, low], axis=0)
    force = jnp.zeros((8, 256), F32)
    for r in range(8):
        out = jnp.dot(three, xn[mk, pl.ds(128 * r, 128), :], preferred_element_type=F32)
        out = out[0:8] + out[8:16] + out[16:24]
        force = force + jnp.where(iota((8, 256), 0) == r, out, 0.0)
    force_ref[...] = jnp.sum(force, axis=0, keepdims=True) / N_S
    leave.append(pltpu.make_async_copy(force_ref, force_hbm, near.at[1]))
    leave[1].start()

    wait(go_a, go_b)
    one = add_inner(ga3[mz], ra3, mz, NZ)
    two = add_inner(gb3[mz], rb3, mz, NZ)
    for h in range(2):
        gram_ref[:, 512 * h : 512 * h + 256] = one[4 * h : 4 * h + 4]
        gram_ref[:, 512 * h + 256 : 512 * h + 512] = two[4 * h : 4 * h + 4]
    leave.append(pltpu.make_async_copy(gram_ref, gram_hbm, near.at[2]))
    leave[2].start()
    wait(*leave)


def deliver(*refs):
    copies = [pltpu.make_async_copy(refs[i], refs[3 + i], refs[6].at[i]) for i in range(3)]
    for copy in copies:
        copy.start()
    wait(*copies)


def body(sample_occ, unique_occ, conn_index, hop_sign, gram_owner, embed, kernels, weights, biases, readout):
    grid = (NZ, NY, NX, 8, 128)
    operands = (
        sample_occ, unique_occ, conn_index, hop_sign, embed, kernels.transpose(1, 0, 2),
        weights, biases, readout.reshape(1, 256),
    )
    results = (
        jax.ShapeDtypeStruct((1, 4), F32),
        jax.ShapeDtypeStruct((4, N_S), F32),
        jax.ShapeDtypeStruct((1, 256), F32),
    )
    made = pl.pallas_call(
        kernel,
        out_shape=results,
        in_specs=[pl.BlockSpec(memory_space=pl.ANY)] * 10,
        out_specs=(pl.BlockSpec(memory_space=pl.ANY),) * 3,
        scratch_shapes=[
            pltpu.SMEM((256,), jnp.int32),
            pltpu.VMEM((1, 4), F32),
            pltpu.VMEM((4, N_S), F32),
            pltpu.VMEM((1, 256), F32),
        ]
        + [pltpu.VMEM(v.shape, v.dtype) for v in operands]
        + [
            pltpu.VMEM((8, 256, 128), BF16),
            pltpu.VMEM((160, 512), BF16),
            pltpu.VMEM((12, 16, 128), F32),
            pltpu.VMEM((20, 16, 128), F32),
            pltpu.VMEM((12, 16, 8, 256), F32),
            pltpu.VMEM((20, 16, 8, 256), F32),
            pltpu.VMEM((25, 8, 256), F32),
            pltpu.VMEM((2, 128, 256), BF16),
            pltpu.VMEM((8, 256), F32),
            pltpu.VMEM((2, 1024, 128), F32),
            pltpu.VMEM((2, 1024, 128), F32),
            pltpu.VMEM((2, 2048, 128), F32),
            pltpu.VMEM((2, 256, 8, 128), F32),
            pltpu.VMEM((2, 1024, 256), BF16),
            pltpu.VMEM((2, 128, 8, 256), F32),
            pltpu.VMEM((32, 128), F32),
            pltpu.VMEM((5, 256, 128), F32),
            pltpu.VMEM((2, 8, 128), F32),
        ]
        + [pltpu.VMEM(grid, BF16)] * 6
        + [pltpu.VMEM((NZ, NY, NK, NX, 8, 128), BF16)] * 3
        + [pltpu.VMEM((2048, 128), F32)]
        + [pltpu.VMEM((NZ, NY, NX, 8, 256), BF16)] * 2
        + [pltpu.VMEM((4, NZ, 4, 8, 256), BF16)] * 2
        + [pltpu.VMEM((NZ, 4, 8, 256), BF16)] * 2
        + [pltpu.VMEM((4, NZ, 8, 256), BF16)] * 2
        + [pltpu.VMEM((NZ, 8, 256), BF16)] * 4
        + [pltpu.VMEM((16, 8, 128), F32)] * 2
        + [pltpu.SemaphoreType.DMA((n,)) for n in (20, 20, 10)],
        compiler_params=pltpu.CompilerParams(
            collective_id=0, has_side_effects=True, vmem_limit_bytes=60 << 20
        ),
        name="local_energy_gram",
    )(gram_owner, *operands)
    energy, gram, force = pl.pallas_call(
        deliver,
        out_shape=results,
        in_specs=[pl.BlockSpec(memory_space=pl.ANY)] * 3,
        out_specs=(pl.BlockSpec(memory_space=pl.ANY),) * 3,
        scratch_shapes=[pltpu.SemaphoreType.DMA((3,))],
        name="deliver",
    )(*made)
    return energy.reshape(4), gram, force.reshape(256)


def solution(mesh):
    both = ("eval", "blk")
    return jax.shard_map(
        body,
        mesh=mesh,
        in_specs=(P(both), P(both), P(both), P(both), P(), P(), P(), P(), P(), P()),
        out_specs=(P(both), P(both), P(both)),
        check_vma=False,
    )
```

```python
import jax
import jax.numpy as jnp
from jax import lax
from jax.experimental import pallas as pl
from jax.experimental.pallas import tpu as pltpu
from jax.sharding import PartitionSpec as P

MESH = pl.DeviceIdType.MESH
PLANES = (("z", "k"), ("y", "x"))
F32 = jnp.float32
BF16 = jnp.bfloat16
NZ, NY, NX, NK = 8, 4, 4, 2
N_S = 1024
WORK = (8, 3, 3, 3, 6, 1)
T0 = (((0,), (0,)), ((), ()))
NT = (((1,), (1,)), ((), ()))


def iota(shape, dim):
    return lax.broadcasted_iota(jnp.int32, shape, dim)


def spread_table(spread_ref):
    site, lane = iota((256, 128), 0), iota((256, 128), 1)
    same = lax.rem(site, 16) == lax.div(lane, 8)
    for c in range(8):
        hit = jnp.logical_and(same, lax.rem(lane, 8) == c)
        spread_ref[c] = jnp.where(hit, 1.0, 0.0).astype(BF16)


def occupied(occ_ref, first, spread_ref, rows, split):
    total = None
    sub, lane = iota((1, 8, 256), 1), iota((rows, 8, 256), 2)
    for c in range(8):
        o = occ_ref[first + (c % 4 if split else c)].astype(F32)
        o = jnp.where(lax.rem(sub, 2) == 0, o[0:1, :][None], o[1:2, :][None])
        row = lax.rem(iota((rows, 8, 256), 0) + (14 + (8 * (c // 4) if split else 0)), 16)
        o = jnp.where(lax.div(lane, 16) == row, o, 0.0).reshape(rows * 8, 256).astype(BF16)
        part = jnp.dot(o, spread_ref[c], preferred_element_type=F32)
        total = part if total is None else total + part
    return total.reshape(rows, 8, 128)


def patch_rows(t, zed_ref, rows):
    sub = iota((rows, 8, 128), 1)
    r = [t if dy == 2 else pltpu.roll(t, (8 * (2 - dy)) % 128, 2) for dy in range(5)]
    first = jnp.where(sub < 2, r[0], jnp.where(sub < 4, r[1], jnp.where(sub < 6, r[2], r[3])))
    second = jnp.where(sub < 2, r[4], jnp.where(sub == 2, 1.0, 0.0))
    zed_ref[:, 0:8, :] = first
    zed_ref[:, 8:16, :] = second


def tap_weights(embed_ref, k_ref, wz_ref):
    sub = iota((8, 256), 0)
    spin = jnp.where(lax.rem(sub, 2) == 0, embed_ref[0:1, :], embed_ref[1:2, :])
    const = embed_ref[2:3, :] * jnp.sum(k_ref[...], axis=0)[0:1, :]
    for dx in range(5):
        k = [k_ref[dx * 5 + dy, 0:1, :] for dy in range(5)]
        top = jnp.where(sub < 2, k[0], jnp.where(sub < 4, k[1], jnp.where(sub < 6, k[2], k[3]))) * spin
        low = jnp.where(sub < 2, k[4] * spin, jnp.where(sub == 2, const, 0.0) if dx == 0 else 0.0)
        own = jnp.where(lax.div(sub, 2) == 2, spin, 0.0) if dx == 2 else jnp.zeros((8, 256), F32)
        one = jnp.where(sub == 2, embed_ref[2:3, :], 0.0) if dx == 0 else jnp.zeros((8, 256), F32)
        base = jnp.concatenate(
            [jnp.concatenate([top, low], axis=0), jnp.concatenate([own, one], axis=0)], axis=1
        )
        high = base.astype(BF16)
        wz_ref[16 * dx : 16 * dx + 16, :] = high
        wz_ref[80 + 16 * dx : 96 + 16 * dx, :] = (base - high.astype(F32)).astype(BF16)


def first_layer(zed_ref, wz_ref, w_ref, b_ref, state_ref, low, high):
    many = 4

    def step(i, carry):
        xs = [i * many + k for k in range(many)]
        cols = []
        for x in xs:
            taps = [zed_ref[x + j].astype(BF16) for j in range(5)]
            cols.append(jnp.concatenate(taps + taps, axis=0))
        cols = jnp.concatenate(cols, axis=1)
        both = lax.dot_general(cols, wz_ref[...], T0, preferred_element_type=F32)
        mixed = both[:, :256].astype(BF16)
        pre = jnp.dot(mixed, w_ref[0], preferred_element_type=F32) + b_ref[0:1, :]
        half = 0.5 * pre
        new = both[:, 256:] + (half + half * jnp.tanh(half))
        state_ref[pl.ds(i * many + 2, many)] = new.reshape(many, 16, 8, 256)
        return carry

    lax.fori_loop(low // many, high // many, step, 0)


def halo(state_ref, rows, swap):
    for i in (0, 1):
        low = state_ref[rows + i]
        high = state_ref[2 + i]
        if swap:
            low = pltpu.roll(low, 4, 1)
            high = pltpu.roll(high, 4, 1)
        state_ref[i] = low
        state_ref[rows + 2 + i] = high


def convolve(state_ref, kb_ref, x):
    halves = []
    for h in range(2):
        lanes = slice(128 * h, 128 * h + 128)
        acc = None
        for dx in range(5):
            row = state_ref[x + dx, :, :, lanes]
            for dy in range(5):
                s = (dy - 2) % 16
                moved = row if s == 0 else jnp.concatenate([row[s:], row[:s]], axis=0)
                term = moved * kb_ref[dx * 5 + dy, :, lanes][None]
                acc = term if acc is None else acc + term
        halves.append(acc.reshape(128, 128))
    return jnp.concatenate(halves, axis=1)


class SecondLayer:
    def __init__(self, state_ref, kb_ref, mix_ref, w_ref, b_ref, total_ref, rows, keep_mixed=None, keep_rest=None):
        self.state, self.kb, self.mix, self.w, self.b = state_ref, kb_ref, mix_ref, w_ref, b_ref
        self.total, self.rows, self.keep_mixed, self.keep_rest = total_ref, rows, keep_mixed, keep_rest

    def finish(self, x, total):
        pre = jnp.dot(self.mix[lax.rem(x, 2)], self.w[1], preferred_element_type=F32) + self.b[1:2, :]
        half = 0.5 * pre
        th_half = jnp.tanh(half)
        out = jnp.tanh(self.state[x + 2].reshape(128, 256) + (half + half * th_half))
        if self.keep_rest is not None:
            self.keep_rest(x, pre, th_half, out)
        return total + jnp.sum(out.reshape(16, 8, 256), axis=0)

    def make(self, x):
        mixed = convolve(self.state, self.kb, x)
        self.mix[lax.rem(x, 2)] = mixed.astype(BF16)
        if self.keep_mixed is not None:
            self.keep_mixed(x, mixed)

    def part(self, low, high):
        if low == 0:
            self.make(jnp.int32(0))
            self.total[...] = jnp.zeros((8, 256), F32)

        def step(x, total):
            total = self.finish(x - 1, total)
            self.make(x)
            return total

        total = lax.fori_loop(max(low, 1), high, step, self.total[...])
        self.total[...] = self.finish(jnp.int32(high - 1), total) if high == self.rows else total


class Wire:
    def __init__(self, send, recv):
        e, x = lax.axis_index("eval"), lax.axis_index("blk")
        self.at = {
            "z": lax.div(e, NY * NK),
            "y": lax.rem(lax.div(e, NK), NY),
            "k": lax.rem(e, NK),
            "x": x,
        }
        self.size = {"z": NZ, "y": NY, "k": NK, "x": NX}
        self.send, self.recv, self.used = send, recv, 0

    def linear(self):
        return ((self.at["z"] * NY + self.at["y"]) * NK + self.at["k"]) * NX + self.at["x"]

    def peer(self, axis, off):
        return lax.rem(self.at[axis] + off, self.size[axis])

    def device(self, axis, place):
        at = {**self.at, axis: place}
        return ((at["z"] * NY + at["y"]) * NK + at["k"], at["x"])

    def member(self, axes, place):
        inner = self.size[axes[1]]
        at = {**self.at, axes[0]: lax.div(place, inner), axes[1]: lax.rem(place, inner)}
        return ((at["z"] * NY + at["y"]) * NK + at["k"], at["x"])

    def rank(self, axes):
        return self.at[axes[0]] * self.size[axes[1]] + self.at[axes[1]]

    def greet(self):
        sem = pltpu.get_barrier_semaphore()
        count = 0
        for axes in PLANES:
            many = self.size[axes[0]] * self.size[axes[1]]
            for off in range(1, many):
                place = lax.rem(self.rank(axes) + off, many)
                pl.semaphore_signal(sem, inc=1, device_id=self.member(axes, place), device_id_type=MESH)
                count += 1
        return sem, count

    def pair(self):
        self.used += 1
        return {"send_sem": self.send.at[self.used - 1], "recv_sem": self.recv.at[self.used - 1]}

    def end(self, sems, region, device):
        return pltpu.make_async_remote_copy(
            src_ref=region, dst_ref=region, device_id=device, device_id_type=MESH, **sems
        )

    def share(self, axes, src, dst_ref):
        many = self.size[axes[0]] * self.size[axes[1]]
        sems = self.pair()
        for off in range(1, many):
            device = self.member(axes, lax.rem(self.rank(axes) + off, many))
            pltpu.make_async_remote_copy(
                src_ref=src, dst_ref=dst_ref.at[self.rank(axes)], device_id=device, device_id_type=MESH, **sems
            ).start()
        return self.end(sems, dst_ref.at[0 : many - 1], device)

    def push(self, axis, src, dst, sems):
        for off in range(1, self.size[axis]):
            place = self.peer(axis, off)
            pltpu.make_async_remote_copy(
                src_ref=src(place),
                dst_ref=dst(self.at[axis]),
                device_id=self.device(axis, place),
                device_id_type=MESH,
                **sems,
            ).start()

    def start(self, axis, src, dst):
        sems = self.pair()
        self.push(axis, src, dst, sems)
        return self.end(sems, dst(pl.ds(0, self.size[axis] - 1)), self.device(axis, self.peer(axis, 1)))


def wait(*groups):
    for group in groups:
        group.wait()


def jacobian(mixf_ref, cotf_ref, jf_ref):
    for s in range(4):
        rows = pl.ds(s, 256, stride=4)
        left = jnp.concatenate([mixf_ref[h, rows, :] for h in range(2)], axis=1).astype(BF16)
        right = jnp.concatenate([cotf_ref[h, rows, :] for h in range(2)], axis=1).astype(BF16)
        out = lax.dot_general(left, right, T0, preferred_element_type=F32)
        for h in range(2):
            jf_ref[h, pl.ds(s, 256, stride=8), :] = out[:, 128 * h : 128 * h + 128]


def lay_out(jf_ref, h, send_ref):
    low = iota((NY, NX, 8, 128), 2) < 4
    for z in range(NZ):
        t = jf_ref[h, z * 256 : z * 256 + 256, :].reshape(NY, NK, NX, 8, 128)
        send_ref[z] = jnp.where(low, t[:, 0], pltpu.roll(t[:, 1], 4, 2)).astype(BF16)


def core_sum(full_ref, core):
    def add(z, total):
        return total + jnp.sum(full_ref[z, :, core].reshape(NY * NX, 8, 128).astype(F32), axis=0)

    return lax.fori_loop(0, NZ, add, jnp.zeros((8, 128), F32))


def center(full_refs, totals, xc_ref, xn_ref):
    for h in range(2):
        total = totals[h]
        means = [jnp.sum(total[4 * k : 4 * k + 4], axis=0, keepdims=True) / N_S for k in range(2)]
        mean = jnp.where(iota((8, 128), 0) < 4, means[0], means[1])

        def step(z, carry):
            t = full_refs[h][z].reshape(32, 8, 128).astype(F32) - mean[None]
            t = t.astype(BF16).astype(F32)
            xc_ref[h, pl.ds(z * 32, 32)] = t
            t = t.reshape(16, 2, 8, 128)
            low = iota((16, 8, 128), 1) < 4
            one = jnp.where(low, t[:, 0], pltpu.roll(t[:, 1], 4, 1))
            two = jnp.where(low, pltpu.roll(t[:, 0], 4, 1), t[:, 1])
            for k, v in enumerate((one, two)):
                v = v.reshape(128, 128)
                xn_ref[k, pl.ds(z * 128, 128), 128 * h : 128 * h + 128] = v.astype(BF16)
            return carry

        lax.fori_loop(0, NZ, step, 0)


def gram_rows(owner_ref, core, xc_ref, left_ref):
    low = iota((8, 128), 0) < 4

    def step(i, carry):
        for j in range(16):
            q = i * 16 + j
            own = owner_ref[i * (2 * NK * NX * 2) + (j // NX) * (NK * NX) + core * NX + j % NX]
            for h in range(2):
                t = xc_ref[h, own]
                r = pltpu.roll(t, 4, 0)
                left_ref[0, q, :, 128 * h : 128 * h + 128] = jnp.where(low, t, r)
                left_ref[1, q, :, 128 * h : 128 * h + 128] = jnp.where(low, r, t)
        return carry

    lax.fori_loop(0, NZ, step, 0)


def gram_part(left_ref, xn_ref, out_ref, c):
    low = lax.rem(lax.div(iota((N_S, 256), 0), 4), 2) == 0
    rows = [left_ref[k].reshape(N_S, 256).astype(BF16) for k in range(2)]
    both = []
    for first in (256 * c, 256 * c + 512):
        out = None
        for k in range(2):
            part = lax.dot_general(rows[k], xn_ref[k, first : first + 256, :], NT, preferred_element_type=F32)
            out = part if out is None else out + part
        both.append(out)
    out = jnp.where(low, both[0], both[1]) * (1.0 / N_S)
    out_ref[...] = out.astype(BF16).reshape(NZ, NY, NX, 8, 256)


def add_outer(own, got_ref, out_ref, at, size):
    def step(z, carry):
        total = own(z).astype(F32)
        for off in range(1, size):
            total = total + got_ref[lax.rem(at + off, size), z].astype(F32)
        out_ref[z] = total.astype(BF16)
        return carry

    lax.fori_loop(0, NZ, step, 0)


def add_inner(own, got_ref, at, size):
    total = own.astype(F32)
    for off in range(1, size):
        total = total + got_ref[lax.rem(at + off, size)].astype(F32)
    return total


def own_info(index_ref, sign_ref, occ_ref, amp):
    sub, lane = iota((4, 128), 0), iota((4, 128), 1)
    pick = jnp.where(iota((32, 128), 0) == lax.div(iota((32, 128), 1), 4), 1.0, 0.0).astype(BF16)
    mine = sub == lax.rem(lane, 4)

    def row(v):
        v = jnp.dot(v.astype(F32).astype(BF16), pick, preferred_element_type=F32)
        return jnp.sum(jnp.where(mine, v, 0.0), axis=0, keepdims=True)

    index = index_ref[...]
    rows = [row(lax.shift_right_logical(index, 5)), row(jnp.bitwise_and(index, 31)), row(2 * sign_ref[...] - 1)]
    whole = jnp.sum(jnp.where(iota((8, 128), 0) == lax.rem(iota((8, 128), 1), 4), amp, 0.0), axis=0, keepdims=True)
    for _ in range(3):
        part = whole.astype(BF16).astype(F32)
        rows.append(part)
        whole = whole - part
    site = jnp.zeros((1, 128), F32)
    for i in range(4):
        o = occ_ref[i].astype(F32) - 0.5
        value = 4.0 * jnp.sum(o[0:1, :] * o[1:2, :], axis=1, keepdims=True)
        site = jnp.where(lax.rem(iota((1, 128), 1), 4) == i, value, site)
    rows += [site, jnp.zeros((1, 128), F32)]
    return jnp.concatenate(rows, axis=0).astype(BF16)


def kernel(
    owner_hbm, occ_s_hbm, occ_u_hbm, index_hbm, sign_hbm, embed_hbm, k_hbm, w_hbm, b_hbm, ro_hbm,
    energy_hbm, gram_hbm, force_hbm,
    owner_ref, energy_ref, gram_ref, force_ref, occ_s_ref, occ_u_ref, index_ref, sign_ref, embed_ref, k_ref, w_ref, b_ref, ro_ref,
    spread, wz, zs, zu, ss, su, kb, mix, sums, mixf, cotf, jf, xc, xn, left, uv, dense, part,
    a0, a1, a2, b0, b1, b2, fa, fb, ag, agf,
    ga, gb, ra1, rb1, ga2, gb2, ra2, rb2, ga3, gb3, ra3, rb3,
    ar_one, ar_two,
    send, recv, near,
):
    wire = Wire(send, recv)
    mz, my, mk, mx = (wire.at[a] for a in "zykx")
    fetched = [
        pltpu.make_async_copy(src, dst, near.at[i])
        for i, (src, dst) in enumerate(
            (
                (k_hbm, k_ref), (embed_hbm, embed_ref), (occ_s_hbm, occ_s_ref), (b_hbm, b_ref), (ro_hbm, ro_ref),
                (w_hbm, w_ref), (occ_u_hbm, occ_u_ref), (index_hbm, index_ref), (sign_hbm, sign_ref), (owner_hbm, owner_ref),
            )
        )
    ]
    for copy in fetched:
        copy.start()
    entry, count = wire.greet()
    spread_table(spread)
    for copy in fetched[:6]:
        copy.wait()
    for t in range(25):
        kb[t] = jnp.broadcast_to(k_ref[t, 1:2, :], (8, 256))
    tap_weights(embed_ref, k_ref, wz)

    patch_rows(occupied(occ_s_ref, 0, spread, 12, True), zs, 12)
    first_layer(zs, wz, w_ref, b_ref, ss, 0, 8)
    halo(ss, 8, True)

    def keep_mixed(x, mixed):
        for h in range(2):
            mixf[h, pl.ds(x * 128, 128), :] = mixed[:, 128 * h : 128 * h + 128].astype(BF16).astype(F32)

    def keep_cot(x, pre, th, out):
        g = 0.5 + 0.5 * th
        cot = ro_ref[...] * (1.0 - out * out) * (g * (1.0 + pre * (1.0 - g)))
        for h in range(2):
            cotf[h, pl.ds(x * 128, 128), :] = cot[:, 128 * h : 128 * h + 128].astype(BF16).astype(F32)

    SecondLayer(ss, kb, mix, w_ref, b_ref, sums, 8, keep_mixed, keep_cot).part(0, 8)
    jacobian(mixf, cotf, jf)
    lay_out(jf, 0, a0)
    for copy in fetched[6:]:
        copy.wait()
    pl.semaphore_wait(entry, count)

    go_a = wire.start("z", lambda p: a0.at[p], lambda p: a1.at[p])
    lay_out(jf, 1, b0)
    go_b = wire.start("y", lambda p: b0.at[:, p], lambda p: b1.at[:, p])
    amp = jnp.broadcast_to(jnp.sum(sums[...] * ro_ref[...], axis=1, keepdims=True), (8, 128))
    amp = amp + pltpu.roll(amp, 4, 0)
    ag[mz, my, mk, mx] = own_info(index_ref, sign_ref, occ_s_ref, amp)
    go_i = wire.start("z", lambda p: ag.at[mz, my, mk, mx], lambda p: ag.at[p, my, mk, mx])
    a1[mz] = a0[mz]
    b1[:, my] = b0[:, my]

    layer = SecondLayer(su, kb, mix, w_ref, b_ref, sums, 16)

    def unique():
        for g in range(4):
            patch_rows(occupied(occ_u_ref, 8 * g, spread, 20, False), zu, 20)
            yield
            first_layer(zu, wz, w_ref, b_ref, su, 0, 8)
            yield
            first_layer(zu, wz, w_ref, b_ref, su, 8, 16)
            halo(su, 16, False)
            yield
            for x in range(0, 16, 4):
                layer.part(x, x + 4)
                if x == 12:
                    uv[8 * g : 8 * g + 8, :] = jnp.broadcast_to(
                        jnp.sum(sums[...] * ro_ref[...], axis=1, keepdims=True), (8, 128)
                    )
                yield

    pieces = unique()

    def work(n):
        for _ in range(n):
            next(pieces, None)

    work(WORK[0])
    wait(go_b, go_i)
    go_b = wire.start("x", lambda p: b1.at[:, :, p], lambda p: b2.at[:, :, p])
    go_i = wire.start("x", lambda p: ag.at[:, my, mk, mx], lambda p: ag.at[:, my, mk, p])
    b2[:, :, mx] = b1[:, :, mx]
    work(WORK[1])
    wait(go_a)
    go_a = wire.start("y", lambda p: a1.at[:, p], lambda p: a2.at[:, p])
    a2[:, my] = a1[:, my]
    work(WORK[2])
    wait(go_b, go_i)
    go_b = wire.start("z", lambda p: b2.at[p], lambda p: fb.at[p, :, mk])
    fb[mz, :, mk] = b2[mz]
    work(WORK[3])
    wait(go_a)
    go_a = wire.start("x", lambda p: a2.at[:, :, p], lambda p: fa.at[:, :, mk, p])
    go_i = wire.start("y", lambda p: ag.at[:, my, mk], lambda p: ag.at[:, p, mk])
    fa[:, :, mk, mx] = a2[:, :, mx]
    work(WORK[4])
    wait(go_a)
    go_a = wire.start("k", lambda p: fa.at[:, :, mk], lambda p: fa.at[:, :, p])
    wait(go_b)
    go_b = wire.start("k", lambda p: fb.at[:, :, mk], lambda p: fb.at[:, :, p])
    totals = [core_sum(full, mk) for full in (fa, fb)]
    work(WORK[5])
    wait(go_i, go_a, go_b)
    go_i = wire.start("k", lambda p: ag.at[:, :, mk], lambda p: ag.at[:, :, p])

    totals = [total + core_sum(full, 1 - mk) for total, full in zip(totals, (fa, fb))]
    center((fa, fb), totals, xc, xn)
    gram_rows(owner_ref, mk, xc, left)
    gram_part(left, xn, ga, 0)
    go_a = wire.start("x", lambda p: ga.at[:, :, p], lambda p: ra1.at[p])
    gram_part(left, xn, gb, 1)
    go_b = wire.start("y", lambda p: gb.at[:, p], lambda p: rb1.at[p])
    wait(go_i)

    def widen(z, carry):
        agf[pl.ds(z * 256, 256), :] = ag[z].reshape(256, 128).astype(F32)
        return carry

    lax.fori_loop(0, NZ, widen, 0)
    for r in range(8):
        rows = pl.ds(32 * r, 32)
        v = [agf[pl.ds(256 * r + row, 32, stride=8), :] for row in range(7)]
        dense[0, rows, :] = v[0]
        dense[1, rows, :] = v[1]
        dense[2, rows, :] = v[2]
        dense[3, rows, :] = v[3] + v[4] + v[5]
        dense[4, rows, :] = v[6]
    work(28)

    mine = wire.linear().astype(F32)
    place = iota((32, 128), 0) == lax.div(iota((32, 128), 1), 4)
    hop, site = [], []
    for r in range(8):
        rows = pl.ds(32 * r, 32)
        local = dense[1, rows, :]
        pick = jnp.zeros((32, 128), F32)
        for u in range(32):
            pick = jnp.where(local == u, uv[u : u + 1, :], pick)
        known = dense[0, rows, :] == mine
        value = jnp.where(known, pick - dense[3, rows, :], 0.0)
        value = jnp.where(known, dense[2, rows, :] * jnp.exp(value), 0.0)
        for shift in (4, 8, 16, 32, 64):
            value = value + pltpu.roll(value, shift, 1)
        hop.append(jnp.sum(jnp.where(place, value, 0.0), axis=0, keepdims=True))
        site.append(jnp.sum(jnp.where(place, dense[4, rows, :], 0.0), axis=0, keepdims=True))
    part[0] = jnp.concatenate(hop, axis=0)
    go_e = wire.share(PLANES[0], part.at[0], ar_one)

    wait(go_a)
    add_outer(lambda z: ga[z, :, mx], ra1, ga2, mx, NX)
    go_a = wire.start("y", lambda p: ga2.at[:, p], lambda p: ra2.at[p])
    wait(go_b)
    add_outer(lambda z: gb[z, my], rb1, gb2, my, NY)
    go_b = wire.start("x", lambda p: gb2.at[:, p], lambda p: rb2.at[p])
    wait(go_e)
    part[1] = add_inner(part[0], ar_one, wire.rank(PLANES[0]), NZ * NK)
    go_e = wire.share(PLANES[1], part.at[1], ar_two)
    wait(go_a)
    ga3[...] = add_inner(ga2[:, my], ra2, my, NY).astype(BF16)
    go_a = wire.start("z", lambda p: ga3.at[p], lambda p: ra3.at[p])
    wait(go_b)
    gb3[...] = add_inner(gb2[:, mx], rb2, mx, NX).astype(BF16)
    go_b = wire.start("z", lambda p: gb3.at[p], lambda p: rb3.at[p])
    wait(go_e)
    hopping = add_inner(part[1], ar_two, wire.rank(PLANES[1]), NY * NX)
    energy = jnp.concatenate(site, axis=0) - hopping
    own = jnp.where(iota((8, 128), 0) == lax.div(wire.linear(), 32), energy, 0.0)
    own = jnp.broadcast_to(jnp.sum(own, axis=0, keepdims=True), (8, 128))
    own = pltpu.roll(own, lax.rem(128 - 4 * lax.rem(wire.linear(), 32), 128), 1)
    energy_ref[...] = own[0:1, 0:4]
    leave = [pltpu.make_async_copy(energy_ref, energy_hbm, near.at[0])]
    leave[0].start()
    shifted = energy - jnp.sum(energy) / N_S
    high = shifted.astype(BF16)
    rest = shifted - high.astype(F32)
    middle = rest.astype(BF16)
    low = (rest - middle.astype(F32)).astype(BF16)
    three = jnp.concatenate([high, middle, low], axis=0)
    force = jnp.zeros((8, 256), F32)
    for r in range(8):
        out = jnp.dot(three, xn[mk, pl.ds(128 * r, 128), :], preferred_element_type=F32)
        out = out[0:8] + out[8:16] + out[16:24]
        force = force + jnp.where(iota((8, 256), 0) == r, out, 0.0)
    force_ref[...] = jnp.sum(force, axis=0, keepdims=True) / N_S
    leave.append(pltpu.make_async_copy(force_ref, force_hbm, near.at[1]))
    leave[1].start()

    wait(go_a, go_b)
    one = add_inner(ga3[mz], ra3, mz, NZ)
    two = add_inner(gb3[mz], rb3, mz, NZ)
    for h in range(2):
        gram_ref[:, 512 * h : 512 * h + 256] = one[4 * h : 4 * h + 4]
        gram_ref[:, 512 * h + 256 : 512 * h + 512] = two[4 * h : 4 * h + 4]
    leave.append(pltpu.make_async_copy(gram_ref, gram_hbm, near.at[2]))
    leave[2].start()
    wait(*leave)


def deliver(*refs):
    copies = [pltpu.make_async_copy(refs[i], refs[3 + i], refs[6].at[i]) for i in range(3)]
    for copy in copies:
        copy.start()
    wait(*copies)


def body(sample_occ, unique_occ, conn_index, hop_sign, gram_owner, embed, kernels, weights, biases, readout):
    grid = (NZ, NY, NX, 8, 128)
    operands = (
        sample_occ, unique_occ, conn_index, hop_sign, embed, kernels.transpose(1, 0, 2),
        weights, biases, readout.reshape(1, 256),
    )
    results = (
        jax.ShapeDtypeStruct((1, 4), F32),
        jax.ShapeDtypeStruct((4, N_S), F32),
        jax.ShapeDtypeStruct((1, 256), F32),
    )
    made = pl.pallas_call(
        kernel,
        out_shape=results,
        in_specs=[pl.BlockSpec(memory_space=pl.ANY)] * 10,
        out_specs=(pl.BlockSpec(memory_space=pl.ANY),) * 3,
        scratch_shapes=[
            pltpu.SMEM((256,), jnp.int32),
            pltpu.VMEM((1, 4), F32),
            pltpu.VMEM((4, N_S), F32),
            pltpu.VMEM((1, 256), F32),
        ]
        + [pltpu.VMEM(v.shape, v.dtype) for v in operands]
        + [
            pltpu.VMEM((8, 256, 128), BF16),
            pltpu.VMEM((160, 512), BF16),
            pltpu.VMEM((12, 16, 128), F32),
            pltpu.VMEM((20, 16, 128), F32),
            pltpu.VMEM((12, 16, 8, 256), F32),
            pltpu.VMEM((20, 16, 8, 256), F32),
            pltpu.VMEM((25, 8, 256), F32),
            pltpu.VMEM((2, 128, 256), BF16),
            pltpu.VMEM((8, 256), F32),
            pltpu.VMEM((2, 1032, 128), F32),
            pltpu.VMEM((2, 1032, 128), F32),
            pltpu.VMEM((2, 2056, 128), F32),
            pltpu.VMEM((2, 256, 8, 128), F32),
            pltpu.VMEM((2, 1024, 256), BF16),
            pltpu.VMEM((2, 128, 8, 256), F32),
            pltpu.VMEM((32, 128), F32),
            pltpu.VMEM((5, 256, 128), F32),
            pltpu.VMEM((2, 8, 128), F32),
        ]
        + [pltpu.VMEM(grid, BF16)] * 6
        + [pltpu.VMEM((NZ, NY, NK, NX, 8, 128), BF16)] * 3
        + [pltpu.VMEM((2056, 128), F32)]
        + [pltpu.VMEM((NZ, NY, NX, 8, 256), BF16)] * 2
        + [pltpu.VMEM((4, NZ, 4, 8, 256), BF16)] * 2
        + [pltpu.VMEM((NZ, 4, 8, 256), BF16)] * 2
        + [pltpu.VMEM((4, NZ, 8, 256), BF16)] * 2
        + [pltpu.VMEM((NZ, 8, 256), BF16)] * 4
        + [pltpu.VMEM((16, 8, 128), F32)] * 2
        + [pltpu.SemaphoreType.DMA((n,)) for n in (20, 20, 10)],
        compiler_params=pltpu.CompilerParams(
            collective_id=0, has_side_effects=True, vmem_limit_bytes=60 << 20
        ),
        name="local_energy_gram",
    )(gram_owner, *operands)
    energy, gram, force = pl.pallas_call(
        deliver,
        out_shape=results,
        in_specs=[pl.BlockSpec(memory_space=pl.ANY)] * 3,
        out_specs=(pl.BlockSpec(memory_space=pl.ANY),) * 3,
        scratch_shapes=[pltpu.SemaphoreType.DMA((3,))],
        name="deliver",
    )(*made)
    return energy.reshape(4), gram, force.reshape(256)


def solution(mesh):
    both = ("eval", "blk")
    return jax.shard_map(
        body,
        mesh=mesh,
        in_specs=(P(both), P(both), P(both), P(both), P(), P(), P(), P(), P(), P()),
        out_specs=(P(both), P(both), P(both)),
        check_vma=False,
    )
```
